32 devices in a mesh: dp: 4 (over y, x), seq: 8 (over z, core).
Axes of the slice: x: 2, y: 2, z: 4, core: 2. Of those that a mesh axis runs over, the one named last changes fastest.
Arguments:
- tokens: float32 [4, 1024, 1024], P('dp', 'seq'), may hold values from -6 to 6
- cotangent: float32 [4, 1024, 1024], P('dp', 'seq'), may hold values from -6 to 6
- doc_ids: int32 [4, 1024], P('dp'), may hold values from 0 to 1, never falling along the last dimension, each value on 1 to 768 neighbouring positions
- in_weight: float32 [1024, 4384], P(('dp', 'seq')), may hold values from -0.1875 to 0.1875
- out_weight: float32 [1024, 2048], P(('dp', 'seq')), may hold values from -0.125 to 0.125
- in_m: float32 [1024, 4384], P(('dp', 'seq')), may hold values from -30 to 30
- in_v: float32 [1024, 4384], P(('dp', 'seq')), may hold values from 1 to 1000
- out_m: float32 [1024, 2048], P(('dp', 'seq')), may hold values from -30 to 30
- out_v: float32 [1024, 2048], P(('dp', 'seq')), may hold values from 1 to 1000
- vec_params: float32 [14688], replicated, as said below
- vec_m: float32 [14688], replicated, may hold values from -30 to 30
- vec_v: float32 [14688], replicated, may hold values from 1 to 1000
Outputs:
- activations: float32 [4, 1024, 1024], P('dp', 'seq')
- input_grad: float32 [4, 1024, 1024], P('dp', 'seq')
- in_grad: float32 [1024, 4384], P(('dp', 'seq'))
- out_grad: float32 [1024, 2048], P(('dp', 'seq'))
- vec_grad: float32 [14688], replicated
- in_new: float32 [1024, 4384], P(('dp', 'seq'))
- out_new: float32 [1024, 2048], P(('dp', 'seq'))
- vec_new: float32 [14688], replicated
- in_m_new: float32 [1024, 4384], P(('dp', 'seq'))
- in_v_new: float32 [1024, 4384], P(('dp', 'seq'))
- out_m_new: float32 [1024, 2048], P(('dp', 'seq'))
- out_v_new: float32 [1024, 2048], P(('dp', 'seq'))
- vec_m_new: float32 [14688], replicated
- vec_v_new: float32 [14688], replicated
The draws below stay inside these ranges and needn't reach their ends.
Inputs may be any that keep to these rules, and one draw needn't show every extreme that they name: `doc_ids`: each row holds document 0 and then document 1, each of one or more positions, none longer than 768. `vec_params`: norm_gain and gate_gain lie in 0.7 to 1.3, skip_gain in 0.5 to 1.5, step_bias in -1 to 1, log_rate in -12 to -3.
All inputs are finite; a program needn't handle non-finite values.
Results may differ from the reference program's by a relative error of at most 0.015.
Values may be sent and summed in bfloat16 or wider, within the bound.
A program may use at most 192 MiB of HBM per device.

```python
import math
import jax
import jax.numpy as jnp
import numpy as np
from jax import lax

D = 1024
DI = 2048
H = 32
P_SIZE = 64
N = 128
KW = 4
STRETCH = 256
STEP = 10
SEQLEN = 1024
SEQS = 4
CONV = 2304
PROJ = 4384
VEC = 14688


def draw_vec_params(key, part):
    subkeys = jax.random.split(key, 7)
    norm_gain = 1.0 + 0.3 * jax.random.uniform(subkeys[0], (D,), jnp.float32, -1.0, 1.0)
    gate_gain = 1.0 + 0.3 * jax.random.uniform(subkeys[1], (DI,), jnp.float32, -1.0, 1.0)
    conv_kernel = 0.5 * jnp.clip(jax.random.normal(subkeys[2], (KW * CONV,), jnp.float32), -4.0, 4.0)
    conv_bias = 0.5 * jnp.clip(jax.random.normal(subkeys[3], (CONV,), jnp.float32), -4.0, 4.0)
    step_bias = jax.random.uniform(subkeys[4], (H,), jnp.float32, -1.0, 1.0)
    log_rate = jax.random.uniform(subkeys[5], (H,), jnp.float32, -10.5, -3.0)
    skip_gain = jax.random.uniform(subkeys[6], (H,), jnp.float32, 0.5, 1.5)
    return jnp.concatenate([norm_gain, gate_gain, conv_kernel, conv_bias, step_bias, log_rate, skip_gain])


def levels(key, shape, cuts, low, largest):
    factor_of = 1.0
    for position, blocks in cuts:
        heights = jax.random.uniform(jax.random.fold_in(jax.random.fold_in(key, 6), position), (blocks,), jnp.float32, low / len(cuts), largest / len(cuts))
        factor_of = factor_of * jnp.repeat(jnp.exp(heights), shape[position] // blocks).reshape((-1,) + (1,) * (len(shape) - 1 - position))
    return factor_of


def profile(amount, total, limit, lean):
    loads = [(1 << 20) // math.isqrt(rank ** lean) + 1 for rank in range(2, amount + 1)]
    spare, given = total - limit - (amount - 1), [1] * (amount - 1)
    while spare > 0:
        movable = [i for i in range(amount - 1) if given[i] < limit]
        whole, budget = sum([loads[i] for i in movable]), spare
        for i in movable:
            extra = min(limit - given[i], max(1, budget * loads[i] // whole), spare)
            given[i] = given[i] + extra
            spare = spare - extra
    return np.array([limit] + given)


def ragged(rng, count, total, most, slope):
    if count == 2:
        one = jax.random.randint(rng, (), max(1, total - most), min(most, total - 1) + 1)
        return jnp.stack([one, total - one])
    tallies = jnp.asarray(profile(count, total, most, slope), jnp.int32)
    couples = (count - 1) // 2
    source_of, taker = tallies[1:1 + 2 * couples:2], tallies[2:2 + 2 * couples:2]
    margin = jnp.minimum(source_of - 1, most - taker)
    moved = jax.random.randint(jax.random.fold_in(rng, 1), (couples,), 0, 1 << 20) % (margin + 1)
    tallies = tallies.at[1:1 + 2 * couples:2].set(source_of - moved).at[2:2 + 2 * couples:2].set(taker + moved)
    return tallies[jax.random.permutation(jax.random.fold_in(rng, 2), count)]


def scatter_about(rng, shape, deviation, limit, cuts=(), held_as=jnp.bfloat16):
    array = jax.random.normal(rng, shape, jnp.float32) * deviation
    if len(cuts) > 0:
        array = levels(rng, shape, cuts, -0.22, 0.18) * array
    return jnp.clip(array, min=-limit, max=limit).astype(held_as)


def setup_inputs(seed: int = 0) -> dict:
    streams_of = jax.random.split(jax.random.key(seed), 13)
    tokens = scatter_about(streams_of[0], (SEQS, SEQLEN, D), 1.0, 6.0, ((0, 4), (1, 8)), jnp.float32)
    cotangent = scatter_about(streams_of[1], (SEQS, SEQLEN, D), 1.0, 6.0, ((0, 4), (1, 8)), jnp.float32)
    doc_ids = jax.vmap(lambda own: jnp.searchsorted(jnp.cumsum(ragged(own, 2, SEQLEN, SEQLEN - SEQLEN // 4, 2)), jnp.arange(SEQLEN), side="right"))(jax.random.split(streams_of[2], SEQS)).reshape((SEQS, SEQLEN)).astype(jnp.int32)
    in_weight = scatter_about(streams_of[3], (D, PROJ), D ** -0.5, 0.1875, ((0, 32),), jnp.float32)
    out_weight = scatter_about(streams_of[4], (D, DI), DI ** -0.5, 0.125, ((0, 32),), jnp.float32)
    in_m = scatter_about(streams_of[5], (D, PROJ), 5.0, 30.0, ((0, 32),), jnp.float32)
    in_v = jnp.clip(jnp.exp(math.log(1000.0) - 6.9077553 * jax.random.uniform(streams_of[6], (D, PROJ), jnp.float32) ** levels(streams_of[6], (D, PROJ), ((0, 32),), -0.2, 0.2)), 1.0, 1000.0)
    out_m = scatter_about(streams_of[7], (D, DI), 5.0, 30.0, ((0, 32),), jnp.float32)
    out_v = jnp.clip(jnp.exp(math.log(1000.0) - 6.9077553 * jax.random.uniform(streams_of[8], (D, DI), jnp.float32) ** levels(streams_of[8], (D, DI), ((0, 32),), -0.2, 0.2)), 1.0, 1000.0)
    vec_params = draw_vec_params(jax.random.fold_in(streams_of[12], 71), 0)
    vec_m = scatter_about(streams_of[10], (VEC,), 5.0, 30.0, (), jnp.float32)
    vec_v = jnp.clip(jnp.exp(jax.random.uniform(streams_of[11], (VEC,), jnp.float32, math.log(1.0), math.log(1000.0))), 1.0, 1000.0)
    return {"tokens": tokens, "cotangent": cotangent, "doc_ids": doc_ids, "in_weight": in_weight, "out_weight": out_weight, "in_m": in_m, "in_v": in_v, "out_m": out_m, "out_v": out_v, "vec_params": vec_params, "vec_m": vec_m, "vec_v": vec_v}


norm_eps = 1e-05
beta_one = 0.9
beta_two = 0.95
learn_rate = 0.03
decay_rate = 0.1
adam_eps = 1e-08
top_precision = lax.Precision.HIGHEST

def unpack(vector):
    cursor = D + DI
    norm_gain = vector[:D]
    gate_gain = vector[D:cursor]
    conv_kernel = vector[cursor:cursor + KW * CONV].reshape(KW, CONV)
    cursor = cursor + KW * CONV
    conv_bias = vector[cursor:cursor + CONV]
    cursor = cursor + CONV
    step_bias = vector[cursor:cursor + H]
    log_rate = vector[cursor + H:cursor + 2 * H]
    skip_gain = vector[cursor + 2 * H:cursor + 3 * H]
    return (norm_gain, gate_gain, conv_kernel, conv_bias, step_bias, log_rate, skip_gain)

def repack(norm_gain, gate_gain, conv_kernel, conv_bias, step_bias, log_rate, skip_gain):
    return jnp.concatenate([norm_gain, gate_gain, conv_kernel.reshape(-1), conv_bias, step_bias, log_rate, skip_gain])

def input_norm(inputs, gain):
    scale = lax.rsqrt(lax.optimization_barrier(jnp.mean(inputs * inputs, axis=-1, keepdims=True)) + norm_eps)
    return inputs * scale * gain[None, :]

def gate_norm(ssd_out, gate_in, gain):
    mixed = ssd_out * jax.nn.silu(gate_in)
    scale = lax.rsqrt(lax.optimization_barrier(jnp.mean(mixed * mixed, axis=-1, keepdims=True)) + norm_eps)
    return mixed * scale * gain[None, :]

def conv_silu(padded, conv_kernel, conv_bias, ext_ids):
    length = padded.shape[0] - (KW - 1)
    own_ids = ext_ids[KW - 1:]
    total = jnp.zeros((length, padded.shape[1]), jnp.float32) + conv_bias[None, :]
    for offset in range(KW):
        valid = (ext_ids[offset:offset + length] == own_ids).astype(jnp.float32)
        total = total + conv_kernel[offset][None, :] * padded[offset:offset + length] * valid[:, None]
    return jax.nn.silu(total)

def rates(step_raw, step_bias, log_rate):
    step_size = jax.nn.softplus(step_raw + step_bias[None, :])
    log_decay = -jnp.exp(log_rate)[None, :] * step_size
    return (step_size, log_decay)

def ssd_block(state, pieces):
    values, input_map, output_map, step_size, log_decay, block_ids, prior_id = pieces
    length = values.shape[0]
    cumulative = jnp.cumsum(log_decay, axis=0)
    rows_index = lax.broadcasted_iota(jnp.int32, (length, length), 0)
    cols_index = lax.broadcasted_iota(jnp.int32, (length, length), 1)
    related = (block_ids[:, None] == block_ids[None, :]) & (rows_index >= cols_index)
    spans = cumulative.T[:, :, None] - cumulative.T[:, None, :]
    decays = jnp.where(related[None], jnp.exp(jnp.where(related[None], spans, 0.0)), 0.0)
    scores = jnp.dot(output_map, input_map.T, precision=top_precision)
    mixing = decays * scores[None] * step_size.T[:, None, :]
    inside = jnp.einsum('hij,jhp->ihp', mixing, values, precision=top_precision)
    carried = (block_ids == prior_id).astype(jnp.float32)
    reach = carried[:, None] * jnp.exp(cumulative)
    entering = jnp.einsum('hpn,in->ihp', state, output_map, precision=top_precision) * reach[:, :, None]
    ending = (block_ids == block_ids[-1]).astype(jnp.float32)
    tail_weight = ending[:, None] * jnp.exp(cumulative[-1][None, :] - cumulative) * step_size
    new_state = state * reach[-1][:, None, None] + jnp.einsum('jh,jhp,jn->hpn', tail_weight, values, input_map, precision=top_precision)
    return (new_state, inside + entering)

def ssd_run(mixed_in, step_size, log_decay, skip_gain, row_ids, prior_id, state, block):
    length = mixed_in.shape[0]
    blocks = length // block
    values = mixed_in[:, :DI].reshape(length, H, P_SIZE)
    input_map = mixed_in[:, DI:DI + N]
    output_map = mixed_in[:, DI + N:]
    shifted = jnp.concatenate([jnp.reshape(prior_id, (1,)).astype(jnp.int32), row_ids[:-1].astype(jnp.int32)])
    priors = shifted.reshape(blocks, block)[:, 0]
    pieces = (values.reshape(blocks, block, H, P_SIZE), input_map.reshape(blocks, block, N), output_map.reshape(blocks, block, N), step_size.reshape(blocks, block, H), log_decay.reshape(blocks, block, H), row_ids.reshape(blocks, block), priors)
    final, outputs = lax.scan(ssd_block, state, pieces)
    result = outputs.reshape(length, H, P_SIZE) + skip_gain[None, :, None] * values
    return (result.reshape(length, DI), final)

def adamw_update(param, grad, first, second):
    first_new = beta_one * first + (1.0 - beta_one) * grad
    second_new = beta_two * second + (1.0 - beta_two) * grad * grad
    corrected = first_new / (1.0 - beta_one ** STEP)
    scaled = jnp.sqrt(second_new / (1.0 - beta_two ** STEP)) + adam_eps
    return (param * (1.0 - learn_rate * decay_rate) - learn_rate * corrected / scaled, first_new, second_new)

def reference(tokens, cotangent, doc_ids, in_weight, out_weight, in_m, in_v, out_m, out_v, vec_params, vec_m, vec_v):
    in_work = in_weight.astype(jnp.bfloat16)
    out_work = out_weight.astype(jnp.bfloat16)
    norm_gain, gate_gain, conv_kernel, conv_bias, step_bias, log_rate, skip_gain = unpack(vec_params)
    block = min(STRETCH, SEQLEN)

    def one_row(totals, row):
        inputs, upstream_f, row_ids = row
        ext_ids = jnp.concatenate([jnp.full((KW - 1,), -1, jnp.int32), row_ids.astype(jnp.int32)])
        normed = input_norm(inputs, norm_gain).astype(jnp.bfloat16)
        projected = jnp.dot(normed, in_work, preferred_element_type=jnp.float32)
        gate_in = projected[:, :DI]
        conv_in = projected[:, DI:DI + CONV].astype(jnp.bfloat16)
        step_raw = projected[:, DI + CONV:]
        padded = jnp.concatenate([jnp.zeros((KW - 1, CONV), jnp.float32), lax.optimization_barrier(conv_in).astype(jnp.float32)])
        mixed_in = lax.optimization_barrier(conv_silu(padded, conv_kernel, conv_bias, ext_ids).astype(jnp.bfloat16)).astype(jnp.float32)

        def ssd_piece(mixed, raw, bias_in, rate_in, skip_in):
            step_size, log_decay = rates(raw, bias_in, rate_in)
            return ssd_run(mixed, step_size, log_decay, skip_in, row_ids, jnp.int32(-1), jnp.zeros((H, P_SIZE, N), jnp.float32), block)[0]
        ssd_out, ssd_back = jax.vjp(ssd_piece, mixed_in, step_raw, step_bias, log_rate, skip_gain)
        gated, gate_back = jax.vjp(gate_norm, ssd_out, gate_in, gate_gain)
        normed_out = gated.astype(jnp.bfloat16)
        outputs = inputs + jnp.dot(normed_out, out_work.T, preferred_element_type=jnp.float32)
        upstream = upstream_f.astype(jnp.bfloat16)
        grad_out_w = jnp.dot(upstream.T, normed_out, preferred_element_type=jnp.float32)
        grad_gated = jnp.dot(upstream, out_work, preferred_element_type=jnp.float32)
        grad_ssd, grad_gate_in, grad_gate_gain = gate_back(grad_gated)
        grad_mixed, grad_raw, grad_bias, grad_rate, grad_skip = ssd_back(grad_ssd)
        _, conv_back = jax.vjp(lambda values, kernel, constant: conv_silu(values, kernel, constant, ext_ids), padded, conv_kernel, conv_bias)
        grad_padded, grad_kernel, grad_cbias = conv_back(grad_mixed)
        grad_proj = jnp.concatenate([grad_gate_in, grad_padded[KW - 1:], grad_raw], axis=1).astype(jnp.bfloat16)
        grad_in_w = jnp.dot(normed.T, grad_proj, preferred_element_type=jnp.float32)
        grad_normed = jnp.dot(grad_proj, in_work.T, preferred_element_type=jnp.float32)
        _, norm_back = jax.vjp(input_norm, inputs, norm_gain)
        grad_inputs, grad_norm_gain = norm_back(grad_normed)
        vector = repack(grad_norm_gain, grad_gate_gain, grad_kernel, grad_cbias, grad_bias, grad_rate, grad_skip)
        totals = (totals[0] + grad_in_w, totals[1] + grad_out_w, totals[2] + vector)
        return (totals, (outputs, upstream_f + grad_inputs))
    start_totals = (jnp.zeros((D, PROJ), jnp.float32), jnp.zeros((D, DI), jnp.float32), jnp.zeros((VEC,), jnp.float32))
    totals, (activations, input_grad) = lax.scan(one_row, start_totals, (tokens, cotangent, doc_ids))
    in_grad, out_grad, vec_grad = totals
    in_new, in_m_new, in_v_new = adamw_update(in_weight, in_grad, in_m, in_v)
    out_new, out_m_new, out_v_new = adamw_update(out_weight, out_grad, out_m, out_v)
    vec_new, vec_m_new, vec_v_new = adamw_update(vec_params, vec_grad, vec_m, vec_v)
    return (activations, input_grad, in_grad, out_grad, vec_grad, in_new, out_new, vec_new, in_m_new, in_v_new, out_m_new, out_v_new, vec_m_new, vec_v_new)
```

```python
import jax
import jax.numpy as jnp
from jax import lax
from jax.experimental import pallas as pl
from jax.experimental.pallas import tpu as pltpu
from jax.sharding import PartitionSpec as P

D = 1024
DI = 2048
H = 32
P_SIZE = 64
N = 128
KW = 4
STRETCH = 256
STEP = 10
CONV = 2304


norm_eps = 1e-05
beta_one = 0.9
beta_two = 0.95
learn_rate = 0.03
decay_rate = 0.1
adam_eps = 1e-08
top_precision = lax.Precision.HIGHEST


def unpack(vector):
    cursor = D + DI
    norm_gain = vector[:D]
    gate_gain = vector[D:cursor]
    conv_kernel = vector[cursor : cursor + KW * CONV].reshape(KW, CONV)
    cursor = cursor + KW * CONV
    conv_bias = vector[cursor : cursor + CONV]
    cursor = cursor + CONV
    step_bias = vector[cursor : cursor + H]
    log_rate = vector[cursor + H : cursor + 2 * H]
    skip_gain = vector[cursor + 2 * H : cursor + 3 * H]
    return (norm_gain, gate_gain, conv_kernel, conv_bias, step_bias, log_rate, skip_gain)


def repack(norm_gain, gate_gain, conv_kernel, conv_bias, step_bias, log_rate, skip_gain):
    return jnp.concatenate(
        [norm_gain, gate_gain, conv_kernel.reshape(-1), conv_bias, step_bias, log_rate, skip_gain]
    )


def input_norm(inputs, gain):
    scale = lax.rsqrt(jnp.mean(inputs * inputs, axis=-1, keepdims=True) + norm_eps)
    return inputs * scale * gain[None, :]


def gate_norm(ssd_out, gate_in, gain):
    mixed = ssd_out * jax.nn.silu(gate_in)
    scale = lax.rsqrt(jnp.mean(mixed * mixed, axis=-1, keepdims=True) + norm_eps)
    return mixed * scale * gain[None, :]


def conv_silu(padded, conv_kernel, conv_bias, ext_ids):
    length = padded.shape[0] - (KW - 1)
    own_ids = ext_ids[KW - 1 :]
    total = jnp.zeros((length, padded.shape[1]), jnp.float32) + conv_bias[None, :]
    for offset in range(KW):
        valid = (ext_ids[offset : offset + length] == own_ids).astype(jnp.float32)
        total = (
            total + conv_kernel[offset][None, :] * padded[offset : offset + length] * valid[:, None]
        )
    return jax.nn.silu(total)


def adamw_update(param, grad, first, second):
    first_new = beta_one * first + (1.0 - beta_one) * grad
    second_new = beta_two * second + (1.0 - beta_two) * grad * grad
    corrected = first_new / (1.0 - beta_one**STEP)
    scaled = jnp.sqrt(second_new / (1.0 - beta_two**STEP)) + adam_eps
    return (
        param * (1.0 - learn_rate * decay_rate) - learn_rate * corrected / scaled,
        first_new,
        second_new,
    )


CHUNK = 128
LANES = 128
bf16 = jnp.bfloat16
f32 = jnp.float32


def contract(a, b, left, right):
    return lax.dot_general(a, b, (((left,), (right,)), ((), ())), preferred_element_type=f32)


def spread_heads(table, heads, length):
    return jnp.concatenate(
        [jnp.broadcast_to(table[:, k : k + 1], (length, P_SIZE)) for k in range(heads)], axis=1
    )


def head_slice(block, k):
    return block[:, k * P_SIZE : (k + 1) * P_SIZE]


def chunk_terms(mixed_ref, raw_ref, meta_ref, ids_ref, small_ref, width):
    length = raw_ref.shape[0]
    values = mixed_ref[:, :width].astype(f32)
    input_map = mixed_ref[:, width : width + N]
    output_map = mixed_ref[:, width + N :]
    shifted_raw = raw_ref[...] + small_ref[0:1, :]
    step_size = jnp.maximum(shifted_raw, 0.0) + jnp.log1p(jnp.exp(-jnp.abs(shifted_raw)))
    rate = -jnp.exp(small_ref[1:2, :])
    log_decay = rate * step_size
    rows_index = lax.broadcasted_iota(jnp.int32, (length, length), 0)
    cols_index = lax.broadcasted_iota(jnp.int32, (length, length), 1)
    lower = rows_index >= cols_index
    cumulative = jnp.dot(
        lower.astype(f32), log_decay, precision=top_precision, preferred_element_type=f32
    )
    flipped = cumulative.T
    same = meta_ref[:, 0:1] == ids_ref[...]
    related = same & lower
    reach = meta_ref[:, 1:2] * jnp.exp(cumulative)
    tail = meta_ref[:, 2:3] * jnp.exp(cumulative[length - 1 :, :] - cumulative)
    scores = contract(output_map, input_map, 1, 1)

    def decay_of(k):
        spans = cumulative[:, k : k + 1] - flipped[k : k + 1, :]
        return jnp.exp(jnp.where(related, spans, -1e30))

    return (values, input_map, output_map, shifted_raw, step_size, rate, log_decay, same,
            rows_index, cols_index, reach, tail, scores, decay_of)


def forward_kernel(heads, mixed_ref, raw_ref, meta_ref, ids_ref, small_ref, out_ref, entry_ref, state):
    width = heads * P_SIZE
    length = raw_ref.shape[0]

    @pl.when(pl.program_id(0) == 0)
    def _():
        state[...] = jnp.zeros_like(state)

    (values, input_map, output_map, _, step_size, _, _, _, _, _, reach, tail, scores, decay_of) = (
        chunk_terms(mixed_ref, raw_ref, meta_ref, ids_ref, small_ref, width)
    )
    entry = state[...]
    entry_low = entry.astype(bf16)
    entry_ref[0] = entry_low
    fed = (values * spread_heads(step_size, heads, length)).astype(bf16)
    inside = []
    for k in range(heads):
        mixing = (scores * decay_of(k)).astype(bf16)
        inside.append(contract(mixing, head_slice(fed, k), 1, 0))
    wide_reach = spread_heads(reach, heads, length)
    out_ref[...] = jnp.concatenate(inside, axis=1) + wide_reach * contract(output_map, entry_low, 1, 0)
    weighted = (fed.astype(f32) * spread_heads(tail, heads, length)).astype(bf16)
    state[...] = entry * wide_reach[length - 1 :, :] + contract(input_map, weighted, 0, 0)


def backward_kernel(heads, mixed_ref, raw_ref, meta_ref, ids_ref, small_ref, skip_ref, ssd_ref,
                    entry_ref, grad_ref, gmix_ref, graw_ref, totals_ref, later, carry):
    width = heads * P_SIZE
    length = raw_ref.shape[0]

    @pl.when(pl.program_id(0) == 0)
    def _():
        later[...] = jnp.zeros_like(later)
        carry[...] = jnp.zeros_like(carry)
        totals_ref[...] = jnp.zeros_like(totals_ref)

    (values, input_map, output_map, shifted_raw, step_size, rate, log_decay, same, rows_index,
     cols_index, reach, tail, scores, decay_of) = chunk_terms(
        mixed_ref, raw_ref, meta_ref, ids_ref, small_ref, width
    )
    grad = grad_ref[...]
    grad_low = grad.astype(bf16)
    wide_step = spread_heads(step_size, heads, length)
    wide_reach = spread_heads(reach, heads, length)
    wide_tail = spread_heads(tail, heads, length)
    fed = (values * wide_step).astype(bf16)
    fed_full = fed.astype(f32)
    after = later[...]
    after_low = after.astype(bf16)
    grad_scores = jnp.zeros((length, length), f32)
    pieces = []
    for k in range(heads):
        decay = decay_of(k)
        mixing = (scores * decay).astype(bf16)
        own_grad = head_slice(grad_low, k)
        grad_scores = grad_scores + contract(own_grad, head_slice(fed, k), 1, 1) * decay
        pieces.append(contract(mixing, own_grad, 0, 0))
    grad_fed = jnp.concatenate(pieces, axis=1) + wide_tail * contract(input_map, after_low, 1, 0)
    reached = (grad * wide_reach).astype(bf16)
    weighted = (fed_full * wide_tail).astype(bf16)
    scores_low = grad_scores.astype(bf16)
    gmix_ref[:, :width] = wide_step * grad_fed + skip_ref[...] * grad
    gmix_ref[:, width : width + N] = contract(scores_low, output_map, 0, 0) + contract(
        weighted, after_low, 1, 1
    )
    gmix_ref[:, width + N :] = contract(scores_low, input_map, 1, 0) + contract(
        reached, entry_ref[0], 1, 1
    )
    later[...] = after * wide_reach[length - 1 :, :] + contract(output_map, reached, 0, 0)
    lane = lax.broadcasted_iota(jnp.int32, (length, LANES), 1)
    balance_wide = grad_low.astype(f32) * ssd_ref[...] - fed_full * grad_fed
    step_wide = values * grad_fed
    skip_wide = values * grad
    balance = jnp.zeros((length, LANES), f32)
    grad_step = jnp.zeros((length, LANES), f32)
    grad_skip = jnp.zeros((length, LANES), f32)
    for k in range(heads):
        here = lane == k
        balance = balance + jnp.where(here, jnp.sum(head_slice(balance_wide, k), axis=1, keepdims=True), 0.0)
        grad_step = grad_step + jnp.where(here, jnp.sum(head_slice(step_wide, k), axis=1, keepdims=True), 0.0)
        grad_skip = grad_skip + jnp.where(here, jnp.sum(head_slice(skip_wide, k), axis=1, keepdims=True), 0.0)
    following = (same & (rows_index <= cols_index)).astype(f32)
    grad_log = jnp.dot(
        following, balance, precision=top_precision, preferred_element_type=f32
    ) + meta_ref[:, 3:4] * carry[0:1, :]
    carry[0:1, :] = grad_log[0:1, :]
    grad_step = grad_step + rate * grad_log
    grad_raw = grad_step * jax.nn.sigmoid(shifted_raw)
    graw_ref[...] = grad_raw
    totals_ref[0:1, :] += jnp.sum(grad_raw, axis=0, keepdims=True)
    totals_ref[1:2, :] += jnp.sum(grad_log * log_decay, axis=0, keepdims=True)
    totals_ref[2:3, :] += jnp.sum(grad_skip, axis=0, keepdims=True)


def ssd_specs(heads, place):
    width = heads * P_SIZE
    return [
        pl.BlockSpec((CHUNK, width + 2 * N), lambda c: (place(c), 0)),
        pl.BlockSpec((CHUNK, LANES), lambda c: (place(c), 0)),
        pl.BlockSpec((CHUNK, 8), lambda c: (place(c), 0)),
        pl.BlockSpec((1, CHUNK), lambda c: (0, place(c))),
        pl.BlockSpec((8, LANES), lambda c: (0, 0)),
    ]


def ssd_forward(heads, mixed, raw, meta, ids_row, small):
    length = mixed.shape[0]
    width = heads * P_SIZE
    count = length // CHUNK
    return pl.pallas_call(
        lambda *refs: forward_kernel(heads, *refs),
        grid=(count,),
        in_specs=ssd_specs(heads, lambda c: c),
        out_specs=[
            pl.BlockSpec((CHUNK, width), lambda c: (c, 0)),
            pl.BlockSpec((1, N, width), lambda c: (c, 0, 0)),
        ],
        out_shape=[
            jax.ShapeDtypeStruct((length, width), f32),
            jax.ShapeDtypeStruct((count, N, width), bf16),
        ],
        scratch_shapes=[pltpu.VMEM((N, width), f32)],
        cost_estimate=pl.CostEstimate(flops=4 * length * N * width, bytes_accessed=4 * length * width, transcendentals=length * CHUNK * heads),
        name="ssd_forward",
    )(mixed, raw, meta, ids_row, small)


def ssd_backward(heads, mixed, raw, meta, ids_row, small, skip, ssd, entries, grad):
    length = mixed.shape[0]
    width = heads * P_SIZE
    count = length // CHUNK
    place = lambda c: count - 1 - c
    return pl.pallas_call(
        lambda *refs: backward_kernel(heads, *refs),
        grid=(count,),
        in_specs=ssd_specs(heads, place)
        + [
            pl.BlockSpec((1, width), lambda c: (0, 0)),
            pl.BlockSpec((CHUNK, width), lambda c: (place(c), 0)),
            pl.BlockSpec((1, N, width), lambda c: (place(c), 0, 0)),
            pl.BlockSpec((CHUNK, width), lambda c: (place(c), 0)),
        ],
        out_specs=[
            pl.BlockSpec((CHUNK, width + 2 * N), lambda c: (place(c), 0)),
            pl.BlockSpec((CHUNK, LANES), lambda c: (place(c), 0)),
            pl.BlockSpec((8, LANES), lambda c: (0, 0)),
        ],
        out_shape=[
            jax.ShapeDtypeStruct((length, width + 2 * N), f32),
            jax.ShapeDtypeStruct((length, LANES), f32),
            jax.ShapeDtypeStruct((8, LANES), f32),
        ],
        scratch_shapes=[pltpu.VMEM((N, width), f32), pltpu.VMEM((8, LANES), f32)],
        cost_estimate=pl.CostEstimate(flops=12 * length * N * width, bytes_accessed=12 * length * width, transcendentals=length * CHUNK * heads),
        name="ssd_backward",
    )(mixed, raw, meta, ids_row, small, skip, ssd, entries, grad)


def position_table(ids):
    chunked = ids.reshape(-1, CHUNK)
    none = jnp.full((1,), -1, jnp.int32)
    prior = jnp.concatenate([none, chunked[:-1, -1]])[:, None]
    following = jnp.concatenate([chunked[1:, 0], none])[:, None]
    last = chunked[:, -1:]
    columns = [chunked, chunked == prior, chunked == last, chunked == following]
    columns = [column.astype(f32).reshape(-1) for column in columns]
    return jnp.stack(columns + [jnp.zeros_like(columns[0])] * 4, axis=1)


def body(tokens, cotangent, doc_ids, in_weight, out_weight, in_m, in_v, out_m, out_v, vec_params, vec_m, vec_v):
    seq_count = lax.axis_size("seq")
    place = lax.axis_index("seq")
    heads = H // seq_count
    width = DI // seq_count
    mixed_width = width + 2 * N
    owner_rows = in_weight.shape[0]
    inputs = tokens[0]
    upstream_f = cotangent[0]
    local_len = inputs.shape[0]
    norm_gain, gate_gain, conv_kernel, conv_bias, step_bias, log_rate, skip_gain = unpack(vec_params)

    def by_place(matrix):
        return matrix.reshape(matrix.shape[0], seq_count, -1).transpose(1, 0, 2)

    in_low = in_weight.astype(bf16)
    out_low = out_weight.astype(bf16)
    shared = jnp.broadcast_to(in_low[None, :, 2 * DI : DI + CONV], (seq_count, owner_rows, 2 * N))
    steps = jnp.pad(by_place(in_low[:, DI + CONV :]), ((0, 0), (0, 0), (0, LANES - heads)))
    blocks = jnp.concatenate(
        [by_place(in_low[:, :DI]), by_place(in_low[:, DI : 2 * DI]), shared, steps, by_place(out_low)], axis=2
    )
    normed = input_norm(inputs, norm_gain).astype(bf16)
    upstream = upstream_f.astype(bf16)
    exchanged = lax.all_to_all(blocks, "seq", 0, 0)
    weights = lax.all_gather(exchanged.reshape(seq_count * owner_rows, -1), "dp", axis=0, tiled=True)
    normed_all = lax.all_gather(normed, "seq", axis=0, tiled=True)
    upstream_all = lax.all_gather(upstream, "seq", axis=0, tiled=True)
    in_width = width + mixed_width + LANES
    in_work = weights[:, :in_width]
    out_work = weights[:, in_width:]

    ids = doc_ids[0]
    ext_ids = jnp.concatenate([jnp.full((KW - 1,), -1, jnp.int32), ids])
    meta = position_table(ids)
    ids_row = ids.astype(f32)[None, :]

    def own(vector, size):
        return lax.dynamic_slice_in_dim(vector, place * size, size, vector.ndim - 1)

    own_gate_gain = own(gate_gain, width)
    own_kernel = jnp.concatenate([own(conv_kernel[:, :DI], width), conv_kernel[:, DI:]], axis=1)
    own_cbias = jnp.concatenate([own(conv_bias[:DI], width), conv_bias[DI:]])
    own_skip = own(skip_gain, heads)
    small = jnp.pad(jnp.stack([own(step_bias, heads), own(log_rate, heads)]), ((0, 6), (0, LANES - heads)))
    wide_skip = jnp.repeat(own_skip, P_SIZE)[None, :]

    projected = jnp.dot(normed_all, in_work, preferred_element_type=f32)
    gate_in = projected[:, :width]
    conv_in = projected[:, width : width + mixed_width].astype(bf16)
    step_raw = projected[:, width + mixed_width :]
    padded = jnp.concatenate([jnp.zeros((KW - 1, mixed_width), bf16), conv_in]).astype(f32)
    mixed = conv_silu(padded, own_kernel, own_cbias, ext_ids).astype(bf16)
    ssd, entries = ssd_forward(heads, mixed, step_raw, meta, ids_row, small)

    grad_gated = jnp.dot(upstream_all, out_work, preferred_element_type=f32)
    values = mixed[:, :width].astype(f32)
    ssd_out = ssd + wide_skip * values
    gate_sig = jax.nn.sigmoid(gate_in)
    gate_act = gate_in * gate_sig
    product = ssd_out * gate_act
    scaled_grad = grad_gated * own_gate_gain[None, :]
    stats = jnp.stack([jnp.sum(product * product, axis=1), jnp.sum(scaled_grad * product, axis=1)])
    stats = lax.psum(stats, "seq")
    raw_out = (product * own_gate_gain[None, :]).astype(bf16)
    out_part = contract(raw_out, out_work, 1, 1).astype(bf16)
    out_sum = lax.psum_scatter(out_part, "seq", scatter_dimension=0, tiled=True).astype(f32)
    scale = lax.rsqrt(stats[0] / DI + norm_eps)
    pull = scale * scale * scale * stats[1] / DI
    own_scale = lax.dynamic_slice_in_dim(scale, place * local_len, local_len)
    outputs = inputs + out_sum * own_scale[:, None]
    grad_product = scaled_grad * scale[:, None] - product * pull[:, None]
    grad_ssd = grad_product * gate_act
    grad_gate_in = grad_product * ssd_out * (gate_sig * (1.0 + gate_in * (1.0 - gate_sig)))
    grad_gate_gain = jnp.sum(grad_gated * product * scale[:, None], axis=0)
    normed_out = (raw_out.astype(f32) * scale[:, None]).astype(bf16)
    out_grad_part = contract(upstream_all, normed_out, 0, 0)

    grad_mixed, grad_raw, totals = ssd_backward(
        heads, mixed, step_raw, meta, ids_row, small, wide_skip, ssd, entries, grad_ssd
    )
    _, conv_back = jax.vjp(
        lambda block, kernel, constant: conv_silu(block, kernel, constant, ext_ids), padded, own_kernel, own_cbias
    )
    grad_padded, grad_kernel, grad_cbias = conv_back(grad_mixed)
    grad_proj = jnp.concatenate([grad_gate_in, grad_padded[KW - 1 :], grad_raw], axis=1).astype(bf16)
    grad_normed_part = contract(grad_proj, in_work, 1, 1).astype(bf16)
    in_grad_part = contract(normed_all, grad_proj, 0, 0)
    grad_normed = lax.psum_scatter(grad_normed_part, "seq", scatter_dimension=0, tiled=True).astype(f32)
    weight_part = jnp.concatenate([in_grad_part, out_grad_part], axis=1).astype(bf16)
    weight_sum = lax.psum_scatter(weight_part, "dp", scatter_dimension=0, tiled=True)
    returned = lax.all_to_all(weight_sum.reshape(seq_count, owner_rows, -1), "seq", 0, 0).astype(f32)

    def gathered(start, size):
        return returned[:, :, start : start + size].transpose(1, 0, 2).reshape(owner_rows, -1)

    in_grad = jnp.concatenate(
        [
            gathered(0, width),
            gathered(width, width),
            jnp.sum(returned[:, :, 2 * width : 2 * width + 2 * N], axis=0),
            gathered(width + mixed_width, heads),
        ],
        axis=1,
    )
    out_grad = gathered(in_width, width)

    grad_norm_gain = jnp.sum(in_work.astype(f32) * in_grad_part, axis=1) / norm_gain

    def placed(part, full, size):
        return lax.dynamic_update_slice_in_dim(
            jnp.zeros(part.shape[:-1] + (full,), f32), part, place * size, part.ndim - 1
        )

    vector = repack(
        grad_norm_gain,
        placed(grad_gate_gain, DI, width),
        jnp.concatenate([placed(grad_kernel[:, :width], DI, width), grad_kernel[:, width:]], axis=1),
        jnp.concatenate([placed(grad_cbias[:width], DI, width), grad_cbias[width:]]),
        placed(totals[0, :heads], H, heads),
        placed(totals[1, :heads], H, heads),
        placed(totals[2, :heads], H, heads),
    )
    vec_grad = lax.psum(vector, ("dp", "seq"))
    _, norm_back = jax.vjp(lambda block: input_norm(block, norm_gain), inputs)
    (grad_inputs,) = norm_back(grad_normed)
    in_new, in_m_new, in_v_new = adamw_update(in_weight, in_grad, in_m, in_v)
    out_new, out_m_new, out_v_new = adamw_update(out_weight, out_grad, out_m, out_v)
    vec_new, vec_m_new, vec_v_new = adamw_update(vec_params, vec_grad, vec_m, vec_v)
    return (
        outputs[None],
        (upstream_f + grad_inputs)[None],
        in_grad,
        out_grad,
        vec_grad,
        in_new,
        out_new,
        vec_new,
        in_m_new,
        in_v_new,
        out_m_new,
        out_v_new,
        vec_m_new,
        vec_v_new,
    )


def solution(mesh):
    in_specs = (
        P("dp", "seq", None),
        P("dp", "seq", None),
        P("dp", None),
        P(("dp", "seq"), None),
        P(("dp", "seq"), None),
        P(("dp", "seq"), None),
        P(("dp", "seq"), None),
        P(("dp", "seq"), None),
        P(("dp", "seq"), None),
        P(),
        P(),
        P(),
    )
    out_specs = (
        P("dp", "seq", None),
        P("dp", "seq", None),
        P(("dp", "seq"), None),
        P(("dp", "seq"), None),
        P(),
        P(("dp", "seq"), None),
        P(("dp", "seq"), None),
        P(),
        P(("dp", "seq"), None),
        P(("dp", "seq"), None),
        P(("dp", "seq"), None),
        P(("dp", "seq"), None),
        P(),
        P(),
    )
    return jax.shard_map(body, mesh=mesh, in_specs=in_specs, out_specs=out_specs, check_vma=False)
```

```python
import jax
import jax.numpy as jnp
from jax import lax
from jax.experimental import pallas as pl
from jax.experimental.pallas import tpu as pltpu
from jax.sharding import PartitionSpec as P

D = 1024
DI = 2048
H = 32
P_SIZE = 64
N = 128
KW = 4
STRETCH = 256
STEP = 10
CONV = 2304


norm_eps = 1e-05
beta_one = 0.9
beta_two = 0.95
learn_rate = 0.03
decay_rate = 0.1
adam_eps = 1e-08
top_precision = lax.Precision.HIGHEST


def unpack(vector):
    cursor = D + DI
    norm_gain = vector[:D]
    gate_gain = vector[D:cursor]
    conv_kernel = vector[cursor : cursor + KW * CONV].reshape(KW, CONV)
    cursor = cursor + KW * CONV
    conv_bias = vector[cursor : cursor + CONV]
    cursor = cursor + CONV
    step_bias = vector[cursor : cursor + H]
    log_rate = vector[cursor + H : cursor + 2 * H]
    skip_gain = vector[cursor + 2 * H : cursor + 3 * H]
    return (norm_gain, gate_gain, conv_kernel, conv_bias, step_bias, log_rate, skip_gain)


def repack(norm_gain, gate_gain, conv_kernel, conv_bias, step_bias, log_rate, skip_gain):
    return jnp.concatenate(
        [norm_gain, gate_gain, conv_kernel.reshape(-1), conv_bias, step_bias, log_rate, skip_gain]
    )


def input_norm(inputs, gain):
    scale = lax.rsqrt(jnp.mean(inputs * inputs, axis=-1, keepdims=True) + norm_eps)
    return inputs * scale * gain[None, :]


def gate_norm(ssd_out, gate_in, gain):
    mixed = ssd_out * jax.nn.silu(gate_in)
    scale = lax.rsqrt(jnp.mean(mixed * mixed, axis=-1, keepdims=True) + norm_eps)
    return mixed * scale * gain[None, :]


def conv_silu(padded, conv_kernel, conv_bias, ext_ids):
    length = padded.shape[0] - (KW - 1)
    own_ids = ext_ids[KW - 1 :]
    total = jnp.zeros((length, padded.shape[1]), jnp.float32) + conv_bias[None, :]
    for offset in range(KW):
        valid = (ext_ids[offset : offset + length] == own_ids).astype(jnp.float32)
        total = (
            total + conv_kernel[offset][None, :] * padded[offset : offset + length] * valid[:, None]
        )
    return jax.nn.silu(total)


def adamw_update(param, grad, first, second):
    first_new = beta_one * first + (1.0 - beta_one) * grad
    second_new = beta_two * second + (1.0 - beta_two) * grad * grad
    corrected = first_new / (1.0 - beta_one**STEP)
    scaled = jnp.sqrt(second_new / (1.0 - beta_two**STEP)) + adam_eps
    return (
        param * (1.0 - learn_rate * decay_rate) - learn_rate * corrected / scaled,
        first_new,
        second_new,
    )


CHUNK = 128
LANES = 128
bf16 = jnp.bfloat16
f32 = jnp.float32


def contract(a, b, left, right):
    return lax.dot_general(a, b, (((left,), (right,)), ((), ())), preferred_element_type=f32)


def spread_heads(table, heads, length):
    return jnp.concatenate(
        [jnp.broadcast_to(table[:, k : k + 1], (length, P_SIZE)) for k in range(heads)], axis=1
    )


def head_slice(block, k):
    return block[:, k * P_SIZE : (k + 1) * P_SIZE]


def chunk_terms(mixed_ref, raw_ref, meta_ref, ids_ref, small_ref, width):
    length = raw_ref.shape[0]
    values = mixed_ref[:, :width].astype(f32)
    input_map = mixed_ref[:, width : width + N]
    output_map = mixed_ref[:, width + N :]
    shifted_raw = raw_ref[...] + small_ref[0:1, :]
    step_size = jnp.maximum(shifted_raw, 0.0) + jnp.log1p(jnp.exp(-jnp.abs(shifted_raw)))
    rate = -jnp.exp(small_ref[1:2, :])
    log_decay = rate * step_size
    rows_index = lax.broadcasted_iota(jnp.int32, (length, length), 0)
    cols_index = lax.broadcasted_iota(jnp.int32, (length, length), 1)
    lower = rows_index >= cols_index
    cumulative = jnp.dot(
        lower.astype(f32), log_decay, precision=top_precision, preferred_element_type=f32
    )
    flipped = cumulative.T
    same = meta_ref[:, 0:1] == ids_ref[...]
    related = same & lower
    reach = meta_ref[:, 1:2] * jnp.exp(cumulative)
    tail = meta_ref[:, 2:3] * jnp.exp(cumulative[length - 1 :, :] - cumulative)
    scores = contract(output_map, input_map, 1, 1)

    def decay_of(k):
        spans = cumulative[:, k : k + 1] - flipped[k : k + 1, :]
        return jnp.exp(jnp.where(related, spans, -1e30))

    return (values, input_map, output_map, shifted_raw, step_size, rate, log_decay, same,
            rows_index, cols_index, reach, tail, scores, decay_of)


def forward_kernel(heads, mixed_ref, raw_ref, meta_ref, ids_ref, small_ref, out_ref, entry_ref, state):
    width = heads * P_SIZE
    length = raw_ref.shape[0]

    @pl.when(pl.program_id(0) == 0)
    def _():
        state[...] = jnp.zeros_like(state)

    (values, input_map, output_map, _, step_size, _, _, _, _, _, reach, tail, scores, decay_of) = (
        chunk_terms(mixed_ref, raw_ref, meta_ref, ids_ref, small_ref, width)
    )
    entry = state[...]
    entry_low = entry.astype(bf16)
    entry_ref[0] = entry_low
    fed = (values * spread_heads(step_size, heads, length)).astype(bf16)
    inside = []
    for k in range(heads):
        mixing = (scores * decay_of(k)).astype(bf16)
        inside.append(contract(mixing, head_slice(fed, k), 1, 0))
    wide_reach = spread_heads(reach, heads, length)
    out_ref[...] = jnp.concatenate(inside, axis=1) + wide_reach * contract(output_map, entry_low, 1, 0)
    weighted = (fed.astype(f32) * spread_heads(tail, heads, length)).astype(bf16)
    state[...] = entry * wide_reach[length - 1 :, :] + contract(input_map, weighted, 0, 0)


def backward_kernel(heads, mixed_ref, raw_ref, meta_ref, ids_ref, small_ref, skip_ref, ssd_ref,
                    entry_ref, grad_ref, gmix_ref, graw_ref, totals_ref, later, carry):
    width = heads * P_SIZE
    length = raw_ref.shape[0]

    @pl.when(pl.program_id(0) == 0)
    def _():
        later[...] = jnp.zeros_like(later)
        carry[...] = jnp.zeros_like(carry)
        totals_ref[...] = jnp.zeros_like(totals_ref)

    (values, input_map, output_map, shifted_raw, step_size, rate, log_decay, same, rows_index,
     cols_index, reach, tail, scores, decay_of) = chunk_terms(
        mixed_ref, raw_ref, meta_ref, ids_ref, small_ref, width
    )
    grad = grad_ref[...]
    grad_low = grad.astype(bf16)
    wide_step = spread_heads(step_size, heads, length)
    wide_reach = spread_heads(reach, heads, length)
    wide_tail = spread_heads(tail, heads, length)
    fed = (values * wide_step).astype(bf16)
    fed_full = fed.astype(f32)
    after = later[...]
    after_low = after.astype(bf16)
    grad_scores = jnp.zeros((length, length), f32)
    pieces = []
    for k in range(heads):
        decay = decay_of(k)
        mixing = (scores * decay).astype(bf16)
        own_grad = head_slice(grad_low, k)
        grad_scores = grad_scores + contract(own_grad, head_slice(fed, k), 1, 1) * decay
        pieces.append(contract(mixing, own_grad, 0, 0))
    grad_fed = jnp.concatenate(pieces, axis=1) + wide_tail * contract(input_map, after_low, 1, 0)
    reached = (grad * wide_reach).astype(bf16)
    weighted = (fed_full * wide_tail).astype(bf16)
    scores_low = grad_scores.astype(bf16)
    gmix_ref[:, :width] = wide_step * grad_fed + skip_ref[...] * grad
    gmix_ref[:, width : width + N] = contract(scores_low, output_map, 0, 0) + contract(
        weighted, after_low, 1, 1
    )
    gmix_ref[:, width + N :] = contract(scores_low, input_map, 1, 0) + contract(
        reached, entry_ref[0], 1, 1
    )
    later[...] = after * wide_reach[length - 1 :, :] + contract(output_map, reached, 0, 0)
    lane = lax.broadcasted_iota(jnp.int32, (length, LANES), 1)
    balance_wide = grad_low.astype(f32) * ssd_ref[...] - fed_full * grad_fed
    step_wide = values * grad_fed
    skip_wide = values * grad
    balance = jnp.zeros((length, LANES), f32)
    grad_step = jnp.zeros((length, LANES), f32)
    grad_skip = jnp.zeros((length, LANES), f32)
    for k in range(heads):
        here = lane == k
        balance = balance + jnp.where(here, jnp.sum(head_slice(balance_wide, k), axis=1, keepdims=True), 0.0)
        grad_step = grad_step + jnp.where(here, jnp.sum(head_slice(step_wide, k), axis=1, keepdims=True), 0.0)
        grad_skip = grad_skip + jnp.where(here, jnp.sum(head_slice(skip_wide, k), axis=1, keepdims=True), 0.0)
    following = (same & (rows_index <= cols_index)).astype(f32)
    grad_log = jnp.dot(
        following, balance, precision=top_precision, preferred_element_type=f32
    ) + meta_ref[:, 3:4] * carry[0:1, :]
    carry[0:1, :] = grad_log[0:1, :]
    grad_step = grad_step + rate * grad_log
    grad_raw = grad_step * jax.nn.sigmoid(shifted_raw)
    graw_ref[...] = grad_raw
    totals_ref[0:1, :] += jnp.sum(grad_raw, axis=0, keepdims=True)
    totals_ref[1:2, :] += jnp.sum(grad_log * log_decay, axis=0, keepdims=True)
    totals_ref[2:3, :] += jnp.sum(grad_skip, axis=0, keepdims=True)


def ssd_specs(heads, place):
    width = heads * P_SIZE
    return [
        pl.BlockSpec((CHUNK, width + 2 * N), lambda c: (place(c), 0)),
        pl.BlockSpec((CHUNK, LANES), lambda c: (place(c), 0)),
        pl.BlockSpec((CHUNK, 8), lambda c: (place(c), 0)),
        pl.BlockSpec((1, CHUNK), lambda c: (0, place(c))),
        pl.BlockSpec((8, LANES), lambda c: (0, 0)),
    ]


def ssd_forward(heads, mixed, raw, meta, ids_row, small):
    length = mixed.shape[0]
    width = heads * P_SIZE
    count = length // CHUNK
    return pl.pallas_call(
        lambda *refs: forward_kernel(heads, *refs),
        grid=(count,),
        in_specs=ssd_specs(heads, lambda c: c),
        out_specs=[
            pl.BlockSpec((CHUNK, width), lambda c: (c, 0)),
            pl.BlockSpec((1, N, width), lambda c: (c, 0, 0)),
        ],
        out_shape=[
            jax.ShapeDtypeStruct((length, width), f32),
            jax.ShapeDtypeStruct((count, N, width), bf16),
        ],
        scratch_shapes=[pltpu.VMEM((N, width), f32)],
        cost_estimate=pl.CostEstimate(flops=4 * length * N * width, bytes_accessed=4 * length * width, transcendentals=length * CHUNK * heads),
        name="ssd_forward",
    )(mixed, raw, meta, ids_row, small)


def ssd_backward(heads, mixed, raw, meta, ids_row, small, skip, ssd, entries, grad):
    length = mixed.shape[0]
    width = heads * P_SIZE
    count = length // CHUNK
    place = lambda c: count - 1 - c
    return pl.pallas_call(
        lambda *refs: backward_kernel(heads, *refs),
        grid=(count,),
        in_specs=ssd_specs(heads, place)
        + [
            pl.BlockSpec((1, width), lambda c: (0, 0)),
            pl.BlockSpec((CHUNK, width), lambda c: (place(c), 0)),
            pl.BlockSpec((1, N, width), lambda c: (place(c), 0, 0)),
            pl.BlockSpec((CHUNK, width), lambda c: (place(c), 0)),
        ],
        out_specs=[
            pl.BlockSpec((CHUNK, width + 2 * N), lambda c: (place(c), 0)),
            pl.BlockSpec((CHUNK, LANES), lambda c: (place(c), 0)),
            pl.BlockSpec((8, LANES), lambda c: (0, 0)),
        ],
        out_shape=[
            jax.ShapeDtypeStruct((length, width + 2 * N), f32),
            jax.ShapeDtypeStruct((length, LANES), f32),
            jax.ShapeDtypeStruct((8, LANES), f32),
        ],
        scratch_shapes=[pltpu.VMEM((N, width), f32), pltpu.VMEM((8, LANES), f32)],
        cost_estimate=pl.CostEstimate(flops=12 * length * N * width, bytes_accessed=12 * length * width, transcendentals=length * CHUNK * heads),
        name="ssd_backward",
    )(mixed, raw, meta, ids_row, small, skip, ssd, entries, grad)


def position_table(ids):
    chunked = ids.reshape(-1, CHUNK)
    none = jnp.full((1,), -1, jnp.int32)
    prior = jnp.concatenate([none, chunked[:-1, -1]])[:, None]
    following = jnp.concatenate([chunked[1:, 0], none])[:, None]
    last = chunked[:, -1:]
    columns = [chunked, chunked == prior, chunked == last, chunked == following]
    columns = [column.astype(f32).reshape(-1) for column in columns]
    return jnp.stack(columns + [jnp.zeros_like(columns[0])] * 4, axis=1)


MESH = pl.DeviceIdType.MESH
in_vmem = pl.BlockSpec(memory_space=pltpu.VMEM)


def beyond(axis, distance):
    count = lax.axis_size(axis)
    return lax.rem(lax.axis_index(axis) + distance + count, count)


def greet(axes):
    barrier = pltpu.get_barrier_semaphore()
    total = 0
    for axis in axes:
        for step in range(1, lax.axis_size(axis)):
            pl.semaphore_signal(barrier, inc=1, device_id={axis: beyond(axis, step)}, device_id_type=MESH)
            total += 1
    pl.semaphore_wait(barrier, total)


def push(source, target, send_sem, recv_sem, axis, peer):
    return pltpu.make_async_remote_copy(
        src_ref=source, dst_ref=target, send_sem=send_sem, recv_sem=recv_sem,
        device_id={axis: peer}, device_id_type=MESH,
    )


def spread_kernel(seq_count, dp_count, blocks, out, seq_send, seq_recv, dp_send, dp_recv):
    here, row = lax.axis_index("seq"), lax.axis_index("dp")
    greet(("seq", "dp"))

    def seq_copy(step, peer, slot):
        return push(blocks.at[peer], out.at[row, slot], seq_send.at[step], seq_recv.at[step], "seq", peer)

    def dp_copy(step, hop, from_row):
        piece = beyond("seq", -step)
        return push(out.at[row, piece], out.at[from_row, piece], dp_send.at[step, hop], dp_recv.at[step, hop], "dp", beyond("dp", hop))

    def launch(step, _):
        seq_copy(step, beyond("seq", step), here).start()
        return 0

    lax.fori_loop(1, seq_count, launch, 0)
    for hop in range(1, dp_count):
        push(blocks.at[here], out.at[row, here], dp_send.at[0, hop], dp_recv.at[0, hop], "dp", beyond("dp", hop)).start()
    out[row, here] = blocks[here]

    def relay(step, _):
        seq_copy(step, beyond("seq", step), beyond("seq", -step)).wait_recv()
        for hop in range(1, dp_count):
            dp_copy(step, hop, row).start()
        return 0

    lax.fori_loop(1, seq_count, relay, 0)

    def finish(step, _):
        for hop in range(1, dp_count):
            copy = dp_copy(step, hop, beyond("dp", -hop))
            copy.wait_recv()
            copy.wait_send()

        @pl.when(step > 0)
        def _():
            seq_copy(step, beyond("seq", step), here).wait_send()

        return 0

    lax.fori_loop(0, seq_count, finish, 0)


def spread_weights(blocks):
    seq_count, dp_count = lax.axis_size("seq"), lax.axis_size("dp")
    sems = pltpu.SemaphoreType.DMA
    return pl.pallas_call(
        lambda *refs: spread_kernel(seq_count, dp_count, *refs),
        out_shape=jax.ShapeDtypeStruct((dp_count,) + blocks.shape, blocks.dtype),
        in_specs=[in_vmem],
        out_specs=in_vmem,
        scratch_shapes=[sems((seq_count,)), sems((seq_count,)), sems((seq_count, dp_count)), sems((seq_count, dp_count))],
        compiler_params=pltpu.CompilerParams(collective_id=1, has_side_effects=True),
        name="spread_weights",
    )(blocks)


def sum_kernel(seq_count, part, out, got, send, recv):
    greet(("seq",))
    copies = [
        push(part, got.at[step], send.at[step], recv.at[step], "seq", beyond("seq", step))
        for step in range(1, seq_count)
    ]
    for copy in copies:
        copy.start()
    got[0] = part[...]
    for copy in copies:
        copy.wait_recv()
    here = lax.axis_index("seq")
    total = got[here]
    for source in range(1, seq_count):
        total = total + got[lax.rem(here - source + seq_count, seq_count)]
    out[...] = total
    for copy in copies:
        copy.wait_send()


def sum_over_seq(part):
    seq_count = lax.axis_size("seq")
    sems = pltpu.SemaphoreType.DMA
    return pl.pallas_call(
        lambda *refs: sum_kernel(seq_count, *refs),
        out_shape=jax.ShapeDtypeStruct(part.shape, part.dtype),
        in_specs=[in_vmem],
        out_specs=in_vmem,
        scratch_shapes=[pltpu.VMEM((seq_count,) + part.shape, part.dtype), sems((seq_count,)), sems((seq_count,))],
        compiler_params=pltpu.CompilerParams(collective_id=2, has_side_effects=True),
        name="sum_over_seq",
    )(part)


def reduce_kernel(seq_count, dp_count, part, vec, returned, vec_out, got, total, vec_dp, vec_row, vec_seq,
                  dp_send, dp_recv, seq_send, seq_recv, va_send, va_recv, vb_send, vb_recv,
                  vc_send, vc_recv, vd_send, vd_recv):
    here, row = lax.axis_index("seq"), lax.axis_index("dp")
    greet(("seq", "dp"))
    hops = range(1, dp_count)
    steps = range(1, seq_count)

    def dp_copy(step, hop):
        piece = beyond("seq", step)
        peer = beyond("dp", hop)
        return push(part.at[peer, piece], got.at[hop, piece], dp_send.at[step, hop], dp_recv.at[step, hop], "dp", peer)

    first = [push(vec.at[beyond("dp", hop)], vec_dp.at[hop], va_send.at[hop], va_recv.at[hop], "dp", beyond("dp", hop)) for hop in hops]
    for copy in first:
        copy.start()

    def launch(step, _):
        for hop in hops:
            dp_copy(lax.rem(step, seq_count), hop).start()
        return 0

    lax.fori_loop(1, seq_count + 1, launch, 0)
    for copy in first:
        copy.wait_recv()
    sums = vec[row]
    for hop in hops:
        sums = sums + vec_dp[hop]
    vec_row[...] = sums
    second = [push(vec_row.at[beyond("seq", step)], vec_seq.at[step], vb_send.at[step], vb_recv.at[step], "seq", beyond("seq", step)) for step in steps]
    for copy in second:
        copy.start()
    for copy in second:
        copy.wait_recv()
    final = vec_row[here]
    for step in steps:
        final = final + vec_seq[step]
    vec_out[row, here] = final

    def third(step, slot):
        return push(vec_out.at[row, here], vec_out.at[row, slot], vc_send.at[step], vc_recv.at[step], "seq", beyond("seq", step))

    for step in steps:
        third(step, here).start()

    def seq_copy(step, slot):
        piece = beyond("seq", step)
        return push(total.at[piece], returned.at[slot], seq_send.at[step], seq_recv.at[step], "seq", piece)

    def combined(step):
        piece = beyond("seq", step)
        for hop in hops:
            dp_copy(step, hop).wait_recv()
        value = part[row, piece].astype(f32)
        for hop in hops:
            value = value + got[hop, piece].astype(f32)
        return value.astype(bf16)

    def exchange(step, _):
        total[beyond("seq", step)] = combined(step)
        seq_copy(step, here).start()
        return 0

    lax.fori_loop(1, seq_count, exchange, 0)
    returned[here] = combined(0)

    for step in steps:
        third(step, beyond("seq", -step)).wait_recv()

    def fourth(hop, slot):
        return push(vec_out.at[row], vec_out.at[slot], vd_send.at[hop], vd_recv.at[hop], "dp", beyond("dp", hop))

    for hop in hops:
        fourth(hop, row).start()

    def finish(step, _):
        seq_copy(step, beyond("seq", -step)).wait_recv()
        seq_copy(step, here).wait_send()
        return 0

    lax.fori_loop(1, seq_count, finish, 0)

    def drain(step, _):
        for hop in hops:
            dp_copy(step, hop).wait_send()
        return 0

    lax.fori_loop(0, seq_count, drain, 0)
    for hop in hops:
        fourth(hop, beyond("dp", -hop)).wait_recv()
        fourth(hop, row).wait_send()
    for copy in first + second:
        copy.wait_send()
    for step in steps:
        third(step, here).wait_send()


def reduce_weights(part, vec):
    seq_count, dp_count = lax.axis_size("seq"), lax.axis_size("dp")
    sems = pltpu.SemaphoreType.DMA
    piece = part.shape[2:]
    lump = vec.shape[2:]
    pairs = [(seq_count, dp_count)] * 2 + [(seq_count,)] * 2 + [(dp_count,)] * 2 + [(seq_count,)] * 4 + [(dp_count,)] * 2
    return pl.pallas_call(
        lambda *refs: reduce_kernel(seq_count, dp_count, *refs),
        out_shape=[jax.ShapeDtypeStruct((seq_count,) + piece, bf16), jax.ShapeDtypeStruct(vec.shape, f32)],
        in_specs=[in_vmem] * 2,
        out_specs=[in_vmem] * 2,
        scratch_shapes=[
            pltpu.VMEM((dp_count, seq_count) + piece, bf16),
            pltpu.VMEM((seq_count,) + piece, bf16),
            pltpu.VMEM((dp_count, seq_count) + lump, f32),
            pltpu.VMEM((seq_count,) + lump, f32),
            pltpu.VMEM((seq_count,) + lump, f32),
        ]
        + [sems(pair) for pair in pairs],
        compiler_params=pltpu.CompilerParams(collective_id=3, has_side_effects=True),
        name="reduce_weights",
    )(part, vec)


def body(tokens, cotangent, doc_ids, in_weight, out_weight, in_m, in_v, out_m, out_v, vec_params, vec_m, vec_v):
    seq_count = lax.axis_size("seq")
    place = lax.axis_index("seq")
    heads = H // seq_count
    width = DI // seq_count
    mixed_width = width + 2 * N
    owner_rows = in_weight.shape[0]
    inputs = tokens[0]
    upstream_f = cotangent[0]
    local_len = inputs.shape[0]
    norm_gain, gate_gain, conv_kernel, conv_bias, step_bias, log_rate, skip_gain = unpack(vec_params)

    def by_place(matrix):
        return matrix.reshape(matrix.shape[0], seq_count, -1).transpose(1, 0, 2)

    in_low = in_weight.astype(bf16)
    out_low = out_weight.astype(bf16)
    shared = jnp.broadcast_to(in_low[None, :, 2 * DI : DI + CONV], (seq_count, owner_rows, 2 * N))
    steps = jnp.pad(by_place(in_low[:, DI + CONV :]), ((0, 0), (0, 0), (0, LANES - heads)))
    blocks = jnp.concatenate(
        [by_place(in_low[:, :DI]), by_place(in_low[:, DI : 2 * DI]), shared, steps, by_place(out_low)], axis=2
    )
    normed = input_norm(inputs, norm_gain).astype(bf16)
    upstream = upstream_f.astype(bf16)
    weights = spread_weights(blocks).reshape(D, -1)
    normed_all = lax.all_gather(normed, "seq", axis=0, tiled=True)
    upstream_all = lax.all_gather(upstream, "seq", axis=0, tiled=True)
    in_width = width + mixed_width + LANES
    in_work = weights[:, :in_width]
    out_work = weights[:, in_width:]

    ids = doc_ids[0]
    ext_ids = jnp.concatenate([jnp.full((KW - 1,), -1, jnp.int32), ids])
    meta = position_table(ids)
    ids_row = ids.astype(f32)[None, :]

    def own(vector, size):
        return lax.dynamic_slice_in_dim(vector, place * size, size, vector.ndim - 1)

    own_gate_gain = own(gate_gain, width)
    own_kernel = jnp.concatenate([own(conv_kernel[:, :DI], width), conv_kernel[:, DI:]], axis=1)
    own_cbias = jnp.concatenate([own(conv_bias[:DI], width), conv_bias[DI:]])
    own_skip = own(skip_gain, heads)
    small = jnp.pad(jnp.stack([own(step_bias, heads), own(log_rate, heads)]), ((0, 6), (0, LANES - heads)))
    wide_skip = jnp.repeat(own_skip, P_SIZE)[None, :]

    projected = jnp.dot(normed_all, in_work, preferred_element_type=f32)
    gate_in = projected[:, :width]
    conv_in = projected[:, width : width + mixed_width].astype(bf16)
    step_raw = projected[:, width + mixed_width :]
    padded = jnp.concatenate([jnp.zeros((KW - 1, mixed_width), bf16), conv_in]).astype(f32)
    mixed = conv_silu(padded, own_kernel, own_cbias, ext_ids).astype(bf16)
    ssd, entries = ssd_forward(heads, mixed, step_raw, meta, ids_row, small)

    grad_gated = jnp.dot(upstream_all, out_work, preferred_element_type=f32)
    values = mixed[:, :width].astype(f32)
    ssd_out = ssd + wide_skip * values
    gate_sig = jax.nn.sigmoid(gate_in)
    gate_act = gate_in * gate_sig
    product = ssd_out * gate_act
    scaled_grad = grad_gated * own_gate_gain[None, :]
    stats = jnp.stack([jnp.sum(product * product, axis=1), jnp.sum(scaled_grad * product, axis=1)])
    stats = sum_over_seq(stats.reshape(-1, LANES)).reshape(2, -1)
    raw_out = (product * own_gate_gain[None, :]).astype(bf16)
    out_part = contract(raw_out, out_work, 1, 1).astype(bf16)
    out_sum = lax.psum_scatter(out_part, "seq", scatter_dimension=0, tiled=True).astype(f32)
    scale = lax.rsqrt(stats[0] / DI + norm_eps)
    pull = scale * scale * scale * stats[1] / DI
    own_scale = lax.dynamic_slice_in_dim(scale, place * local_len, local_len)
    outputs = inputs + out_sum * own_scale[:, None]
    grad_product = scaled_grad * scale[:, None] - product * pull[:, None]
    grad_ssd = grad_product * gate_act
    grad_gate_in = grad_product * ssd_out * (gate_sig * (1.0 + gate_in * (1.0 - gate_sig)))
    grad_gate_gain = jnp.sum(grad_gated * product * scale[:, None], axis=0)
    normed_out = (raw_out.astype(f32) * scale[:, None]).astype(bf16)
    out_grad_part = contract(upstream_all, normed_out, 0, 0)

    grad_mixed, grad_raw, totals = ssd_backward(
        heads, mixed, step_raw, meta, ids_row, small, wide_skip, ssd, entries, grad_ssd
    )
    _, conv_back = jax.vjp(
        lambda block, kernel, constant: conv_silu(block, kernel, constant, ext_ids), padded, own_kernel, own_cbias
    )
    grad_padded, grad_kernel, grad_cbias = conv_back(grad_mixed)
    grad_proj = jnp.concatenate([grad_gate_in, grad_padded[KW - 1 :], grad_raw], axis=1).astype(bf16)
    grad_normed_part = contract(grad_proj, in_work, 1, 1).astype(bf16)
    in_grad_part = contract(normed_all, grad_proj, 0, 0)
    grad_normed = lax.psum_scatter(grad_normed_part, "seq", scatter_dimension=0, tiled=True).astype(f32)
    weight_part = jnp.concatenate([in_grad_part, out_grad_part], axis=1).astype(bf16)
    grad_norm_gain = jnp.sum(in_work.astype(f32) * in_grad_part, axis=1) / norm_gain

    def placed(part, full, size):
        return lax.dynamic_update_slice_in_dim(
            jnp.zeros(part.shape[:-1] + (full,), f32), part, place * size, part.ndim - 1
        )

    vector = repack(
        grad_norm_gain,
        placed(grad_gate_gain, DI, width),
        jnp.concatenate([placed(grad_kernel[:, :width], DI, width), grad_kernel[:, width:]], axis=1),
        jnp.concatenate([placed(grad_cbias[:width], DI, width), grad_cbias[width:]]),
        placed(totals[0, :heads], H, heads),
        placed(totals[1, :heads], H, heads),
        placed(totals[2, :heads], H, heads),
    )
    dp_count = lax.axis_size("dp")
    devices = dp_count * seq_count
    lines = -(-vector.shape[0] // (devices * LANES))
    packed = jnp.pad(vector, (0, devices * lines * LANES - vector.shape[0]))
    returned, vec_sum = reduce_weights(
        weight_part.reshape(dp_count, seq_count, owner_rows, -1), packed.reshape(dp_count, seq_count, lines, LANES)
    )
    returned = returned.astype(f32)
    vec_grad = vec_sum.reshape(-1)[: vector.shape[0]]

    def gathered(start, size):
        return returned[:, :, start : start + size].transpose(1, 0, 2).reshape(owner_rows, -1)

    in_grad = jnp.concatenate(
        [
            gathered(0, width),
            gathered(width, width),
            jnp.sum(returned[:, :, 2 * width : 2 * width + 2 * N], axis=0),
            gathered(width + mixed_width, heads),
        ],
        axis=1,
    )
    out_grad = gathered(in_width, width)

    _, norm_back = jax.vjp(lambda block: input_norm(block, norm_gain), inputs)
    (grad_inputs,) = norm_back(grad_normed)
    in_new, in_m_new, in_v_new = adamw_update(in_weight, in_grad, in_m, in_v)
    out_new, out_m_new, out_v_new = adamw_update(out_weight, out_grad, out_m, out_v)
    vec_new, vec_m_new, vec_v_new = adamw_update(vec_params, vec_grad, vec_m, vec_v)
    return (
        outputs[None],
        (upstream_f + grad_inputs)[None],
        in_grad,
        out_grad,
        vec_grad,
        in_new,
        out_new,
        vec_new,
        in_m_new,
        in_v_new,
        out_m_new,
        out_v_new,
        vec_m_new,
        vec_v_new,
    )


def solution(mesh):
    in_specs = (
        P("dp", "seq", None),
        P("dp", "seq", None),
        P("dp", None),
        P(("dp", "seq"), None),
        P(("dp", "seq"), None),
        P(("dp", "seq"), None),
        P(("dp", "seq"), None),
        P(("dp", "seq"), None),
        P(("dp", "seq"), None),
        P(),
        P(),
        P(),
    )
    out_specs = (
        P("dp", "seq", None),
        P("dp", "seq", None),
        P(("dp", "seq"), None),
        P(("dp", "seq"), None),
        P(),
        P(("dp", "seq"), None),
        P(("dp", "seq"), None),
        P(),
        P(("dp", "seq"), None),
        P(("dp", "seq"), None),
        P(("dp", "seq"), None),
        P(("dp", "seq"), None),
        P(),
        P(),
    )
    return jax.shard_map(body, mesh=mesh, in_specs=in_specs, out_specs=out_specs, check_vma=False)
```

```python
import jax
import jax.numpy as jnp
from jax import lax
from jax.experimental import pallas as pl
from jax.experimental.pallas import tpu as pltpu
from jax.sharding import PartitionSpec as P

D = 1024
DI = 2048
H = 32
P_SIZE = 64
N = 128
KW = 4
STRETCH = 256
STEP = 10
CONV = 2304


norm_eps = 1e-05
beta_one = 0.9
beta_two = 0.95
learn_rate = 0.03
decay_rate = 0.1
adam_eps = 1e-08
top_precision = lax.Precision.HIGHEST


def unpack(vector):
    cursor = D + DI
    norm_gain = vector[:D]
    gate_gain = vector[D:cursor]
    conv_kernel = vector[cursor : cursor + KW * CONV].reshape(KW, CONV)
    cursor = cursor + KW * CONV
    conv_bias = vector[cursor : cursor + CONV]
    cursor = cursor + CONV
    step_bias = vector[cursor : cursor + H]
    log_rate = vector[cursor + H : cursor + 2 * H]
    skip_gain = vector[cursor + 2 * H : cursor + 3 * H]
    return (norm_gain, gate_gain, conv_kernel, conv_bias, step_bias, log_rate, skip_gain)


def repack(norm_gain, gate_gain, conv_kernel, conv_bias, step_bias, log_rate, skip_gain):
    return jnp.concatenate(
        [norm_gain, gate_gain, conv_kernel.reshape(-1), conv_bias, step_bias, log_rate, skip_gain]
    )


def input_norm(inputs, gain):
    scale = lax.rsqrt(jnp.mean(inputs * inputs, axis=-1, keepdims=True) + norm_eps)
    return inputs * scale * gain[None, :]


def gate_norm(ssd_out, gate_in, gain):
    mixed = ssd_out * jax.nn.silu(gate_in)
    scale = lax.rsqrt(jnp.mean(mixed * mixed, axis=-1, keepdims=True) + norm_eps)
    return mixed * scale * gain[None, :]


def conv_silu(padded, conv_kernel, conv_bias, ext_ids):
    length = padded.shape[0] - (KW - 1)
    own_ids = ext_ids[KW - 1 :]
    total = jnp.zeros((length, padded.shape[1]), jnp.float32) + conv_bias[None, :]
    for offset in range(KW):
        valid = (ext_ids[offset : offset + length] == own_ids).astype(jnp.float32)
        total = (
            total + conv_kernel[offset][None, :] * padded[offset : offset + length] * valid[:, None]
        )
    return jax.nn.silu(total)


def adamw_update(param, grad, first, second):
    first_new = beta_one * first + (1.0 - beta_one) * grad
    second_new = beta_two * second + (1.0 - beta_two) * grad * grad
    corrected = first_new / (1.0 - beta_one**STEP)
    scaled = jnp.sqrt(second_new / (1.0 - beta_two**STEP)) + adam_eps
    return (
        param * (1.0 - learn_rate * decay_rate) - learn_rate * corrected / scaled,
        first_new,
        second_new,
    )


CHUNK = 128
LANES = 128
bf16 = jnp.bfloat16
f32 = jnp.float32


def contract(a, b, left, right):
    return lax.dot_general(a, b, (((left,), (right,)), ((), ())), preferred_element_type=f32)


def spread_heads(table, heads, length):
    return jnp.concatenate(
        [jnp.broadcast_to(table[:, k : k + 1], (length, P_SIZE)) for k in range(heads)], axis=1
    )


def head_slice(block, k):
    return block[:, k * P_SIZE : (k + 1) * P_SIZE]


def chunk_terms(mixed_ref, raw_ref, meta_ref, ids_ref, small_ref, width):
    length = raw_ref.shape[0]
    values = mixed_ref[:, :width].astype(f32)
    input_map = mixed_ref[:, width : width + N]
    output_map = mixed_ref[:, width + N :]
    shifted_raw = raw_ref[...] + small_ref[0:1, :]
    step_size = jnp.maximum(shifted_raw, 0.0) + jnp.log1p(jnp.exp(-jnp.abs(shifted_raw)))
    rate = -jnp.exp(small_ref[1:2, :])
    log_decay = rate * step_size
    rows_index = lax.broadcasted_iota(jnp.int32, (length, length), 0)
    cols_index = lax.broadcasted_iota(jnp.int32, (length, length), 1)
    lower = rows_index >= cols_index
    cumulative = jnp.dot(
        lower.astype(f32), log_decay, precision=top_precision, preferred_element_type=f32
    )
    flipped = cumulative.T
    same = meta_ref[:, 0:1] == ids_ref[...]
    related = same & lower
    reach = meta_ref[:, 1:2] * jnp.exp(cumulative)
    tail = meta_ref[:, 2:3] * jnp.exp(cumulative[length - 1 :, :] - cumulative)
    scores = contract(output_map, input_map, 1, 1)

    def decay_of(k):
        spans = cumulative[:, k : k + 1] - flipped[k : k + 1, :]
        return jnp.exp(jnp.where(related, spans, -1e30))

    return (values, input_map, output_map, shifted_raw, step_size, rate, log_decay, same,
            rows_index, cols_index, reach, tail, scores, decay_of)


def forward_kernel(heads, mixed_ref, raw_ref, meta_ref, ids_ref, small_ref, out_ref, entry_ref, state):
    width = heads * P_SIZE
    length = raw_ref.shape[0]

    @pl.when(pl.program_id(0) == 0)
    def _():
        state[...] = jnp.zeros_like(state)

    (values, input_map, output_map, _, step_size, _, _, _, _, _, reach, tail, scores, decay_of) = (
        chunk_terms(mixed_ref, raw_ref, meta_ref, ids_ref, small_ref, width)
    )
    entry = state[...]
    entry_low = entry.astype(bf16)
    entry_ref[0] = entry_low
    fed = (values * spread_heads(step_size, heads, length)).astype(bf16)
    inside = []
    for k in range(heads):
        mixing = (scores * decay_of(k)).astype(bf16)
        inside.append(contract(mixing, head_slice(fed, k), 1, 0))
    wide_reach = spread_heads(reach, heads, length)
    out_ref[...] = jnp.concatenate(inside, axis=1) + wide_reach * contract(output_map, entry_low, 1, 0)
    weighted = (fed.astype(f32) * spread_heads(tail, heads, length)).astype(bf16)
    state[...] = entry * wide_reach[length - 1 :, :] + contract(input_map, weighted, 0, 0)


def backward_kernel(heads, mixed_ref, raw_ref, meta_ref, ids_ref, small_ref, skip_ref, ssd_ref,
                    entry_ref, grad_ref, gmix_ref, graw_ref, totals_ref, later, carry):
    width = heads * P_SIZE
    length = raw_ref.shape[0]

    @pl.when(pl.program_id(0) == 0)
    def _():
        later[...] = jnp.zeros_like(later)
        carry[...] = jnp.zeros_like(carry)
        totals_ref[...] = jnp.zeros_like(totals_ref)

    (values, input_map, output_map, shifted_raw, step_size, rate, log_decay, same, rows_index,
     cols_index, reach, tail, scores, decay_of) = chunk_terms(
        mixed_ref, raw_ref, meta_ref, ids_ref, small_ref, width
    )
    grad = grad_ref[...]
    grad_low = grad.astype(bf16)
    wide_step = spread_heads(step_size, heads, length)
    wide_reach = spread_heads(reach, heads, length)
    wide_tail = spread_heads(tail, heads, length)
    fed = (values * wide_step).astype(bf16)
    fed_full = fed.astype(f32)
    after = later[...]
    after_low = after.astype(bf16)
    grad_scores = jnp.zeros((length, length), f32)
    pieces = []
    for k in range(heads):
        decay = decay_of(k)
        mixing = (scores * decay).astype(bf16)
        own_grad = head_slice(grad_low, k)
        grad_scores = grad_scores + contract(own_grad, head_slice(fed, k), 1, 1) * decay
        pieces.append(contract(mixing, own_grad, 0, 0))
    grad_fed = jnp.concatenate(pieces, axis=1) + wide_tail * contract(input_map, after_low, 1, 0)
    reached = (grad * wide_reach).astype(bf16)
    weighted = (fed_full * wide_tail).astype(bf16)
    scores_low = grad_scores.astype(bf16)
    gmix_ref[:, :width] = wide_step * grad_fed + skip_ref[...] * grad
    gmix_ref[:, width : width + N] = contract(scores_low, output_map, 0, 0) + contract(
        weighted, after_low, 1, 1
    )
    gmix_ref[:, width + N :] = contract(scores_low, input_map, 1, 0) + contract(
        reached, entry_ref[0], 1, 1
    )
    later[...] = after * wide_reach[length - 1 :, :] + contract(output_map, reached, 0, 0)
    channel = lax.broadcasted_iota(jnp.int32, (width, LANES), 0)
    lane = lax.broadcasted_iota(jnp.int32, (width, LANES), 1)
    member = ((channel >= lane * P_SIZE) & (channel < (lane + 1) * P_SIZE)).astype(f32)

    def per_head(wide):
        return jnp.dot(wide, member, precision=top_precision, preferred_element_type=f32)

    balance = per_head(grad_low.astype(f32) * ssd_ref[...] - fed_full * grad_fed)
    grad_step = per_head(values * grad_fed)
    skip_total = per_head(jnp.broadcast_to(jnp.sum(values * grad, axis=0, keepdims=True), (8, width)))
    following = (same & (rows_index <= cols_index)).astype(f32)
    grad_log = jnp.dot(
        following, balance, precision=top_precision, preferred_element_type=f32
    ) + meta_ref[:, 3:4] * carry[0:1, :]
    carry[0:1, :] = grad_log[0:1, :]
    grad_step = grad_step + rate * grad_log
    grad_raw = grad_step * jax.nn.sigmoid(shifted_raw)
    graw_ref[...] = grad_raw
    totals_ref[0:1, :] += jnp.sum(grad_raw, axis=0, keepdims=True)
    totals_ref[1:2, :] += jnp.sum(grad_log * log_decay, axis=0, keepdims=True)
    totals_ref[2:3, :] += skip_total[0:1, :]


def ssd_specs(heads, place):
    width = heads * P_SIZE
    return [
        pl.BlockSpec((CHUNK, width + 2 * N), lambda c: (place(c), 0)),
        pl.BlockSpec((CHUNK, LANES), lambda c: (place(c), 0)),
        pl.BlockSpec((CHUNK, 8), lambda c: (place(c), 0)),
        pl.BlockSpec((1, CHUNK), lambda c: (0, place(c))),
        pl.BlockSpec((8, LANES), lambda c: (0, 0)),
    ]


def ssd_forward(heads, mixed, raw, meta, ids_row, small):
    length = mixed.shape[0]
    width = heads * P_SIZE
    count = length // CHUNK
    return pl.pallas_call(
        lambda *refs: forward_kernel(heads, *refs),
        grid=(count,),
        in_specs=ssd_specs(heads, lambda c: c),
        out_specs=[
            pl.BlockSpec((CHUNK, width), lambda c: (c, 0)),
            pl.BlockSpec((1, N, width), lambda c: (c, 0, 0)),
        ],
        out_shape=[
            jax.ShapeDtypeStruct((length, width), f32),
            jax.ShapeDtypeStruct((count, N, width), bf16),
        ],
        scratch_shapes=[pltpu.VMEM((N, width), f32)],
        cost_estimate=pl.CostEstimate(flops=4 * length * N * width, bytes_accessed=4 * length * width, transcendentals=length * CHUNK * heads),
        name="ssd_forward",
    )(mixed, raw, meta, ids_row, small)


def ssd_backward(heads, mixed, raw, meta, ids_row, small, skip, ssd, entries, grad):
    length = mixed.shape[0]
    width = heads * P_SIZE
    count = length // CHUNK
    place = lambda c: count - 1 - c
    return pl.pallas_call(
        lambda *refs: backward_kernel(heads, *refs),
        grid=(count,),
        in_specs=ssd_specs(heads, place)
        + [
            pl.BlockSpec((1, width), lambda c: (0, 0)),
            pl.BlockSpec((CHUNK, width), lambda c: (place(c), 0)),
            pl.BlockSpec((1, N, width), lambda c: (place(c), 0, 0)),
            pl.BlockSpec((CHUNK, width), lambda c: (place(c), 0)),
        ],
        out_specs=[
            pl.BlockSpec((CHUNK, width + 2 * N), lambda c: (place(c), 0)),
            pl.BlockSpec((CHUNK, LANES), lambda c: (place(c), 0)),
            pl.BlockSpec((8, LANES), lambda c: (0, 0)),
        ],
        out_shape=[
            jax.ShapeDtypeStruct((length, width + 2 * N), f32),
            jax.ShapeDtypeStruct((length, LANES), f32),
            jax.ShapeDtypeStruct((8, LANES), f32),
        ],
        scratch_shapes=[pltpu.VMEM((N, width), f32), pltpu.VMEM((8, LANES), f32)],
        cost_estimate=pl.CostEstimate(flops=12 * length * N * width, bytes_accessed=12 * length * width, transcendentals=length * CHUNK * heads),
        name="ssd_backward",
    )(mixed, raw, meta, ids_row, small, skip, ssd, entries, grad)


def position_table(ids):
    chunked = ids.reshape(-1, CHUNK)
    none = jnp.full((1,), -1, jnp.int32)
    prior = jnp.concatenate([none, chunked[:-1, -1]])[:, None]
    following = jnp.concatenate([chunked[1:, 0], none])[:, None]
    last = chunked[:, -1:]
    columns = [chunked, chunked == prior, chunked == last, chunked == following]
    columns = [column.astype(f32).reshape(-1) for column in columns]
    return jnp.stack(columns + [jnp.zeros_like(columns[0])] * 4, axis=1)


MESH = pl.DeviceIdType.MESH
in_vmem = pl.BlockSpec(memory_space=pltpu.VMEM)


def beyond(axis, distance):
    count = lax.axis_size(axis)
    return lax.rem(lax.axis_index(axis) + distance + count, count)


def greet(axes):
    barrier = pltpu.get_barrier_semaphore()
    total = 0
    for axis in axes:
        for step in range(1, lax.axis_size(axis)):
            pl.semaphore_signal(barrier, inc=1, device_id={axis: beyond(axis, step)}, device_id_type=MESH)
            total += 1
    pl.semaphore_wait(barrier, total)


def push(source, target, send_sem, recv_sem, axis, peer):
    return pltpu.make_async_remote_copy(
        src_ref=source, dst_ref=target, send_sem=send_sem, recv_sem=recv_sem,
        device_id={axis: peer}, device_id_type=MESH,
    )


def spread_kernel(seq_count, dp_count, blocks, out, seq_send, seq_recv, dp_send, dp_recv):
    here, row = lax.axis_index("seq"), lax.axis_index("dp")
    greet(("seq", "dp"))

    def seq_copy(step, peer, slot):
        return push(blocks.at[peer], out.at[row, slot], seq_send.at[step], seq_recv.at[step], "seq", peer)

    def dp_copy(step, hop, from_row):
        piece = beyond("seq", -step)
        return push(out.at[row, piece], out.at[from_row, piece], dp_send.at[step, hop], dp_recv.at[step, hop], "dp", beyond("dp", hop))

    def launch(step, _):
        seq_copy(step, beyond("seq", step), here).start()
        return 0

    lax.fori_loop(1, seq_count, launch, 0)
    for hop in range(1, dp_count):
        push(blocks.at[here], out.at[row, here], dp_send.at[0, hop], dp_recv.at[0, hop], "dp", beyond("dp", hop)).start()
    out[row, here] = blocks[here]

    def relay(step, _):
        seq_copy(step, beyond("seq", step), beyond("seq", -step)).wait_recv()
        for hop in range(1, dp_count):
            dp_copy(step, hop, row).start()
        return 0

    lax.fori_loop(1, seq_count, relay, 0)

    def finish(step, _):
        for hop in range(1, dp_count):
            copy = dp_copy(step, hop, beyond("dp", -hop))
            copy.wait_recv()
            copy.wait_send()

        @pl.when(step > 0)
        def _():
            seq_copy(step, beyond("seq", step), here).wait_send()

        return 0

    lax.fori_loop(0, seq_count, finish, 0)


def spread_weights(blocks):
    seq_count, dp_count = lax.axis_size("seq"), lax.axis_size("dp")
    sems = pltpu.SemaphoreType.DMA
    return pl.pallas_call(
        lambda *refs: spread_kernel(seq_count, dp_count, *refs),
        out_shape=jax.ShapeDtypeStruct((dp_count,) + blocks.shape, blocks.dtype),
        in_specs=[in_vmem],
        out_specs=in_vmem,
        scratch_shapes=[sems((seq_count,)), sems((seq_count,)), sems((seq_count, dp_count)), sems((seq_count, dp_count))],
        compiler_params=pltpu.CompilerParams(collective_id=1, has_side_effects=True),
        name="spread_weights",
    )(blocks)


def sum_kernel(seq_count, part, out, got, send, recv):
    greet(("seq",))
    copies = [
        push(part, got.at[step], send.at[step], recv.at[step], "seq", beyond("seq", step))
        for step in range(1, seq_count)
    ]
    for copy in copies:
        copy.start()
    got[0] = part[...]
    for copy in copies:
        copy.wait_recv()
    here = lax.axis_index("seq")
    total = got[here]
    for source in range(1, seq_count):
        total = total + got[lax.rem(here - source + seq_count, seq_count)]
    out[...] = total
    for copy in copies:
        copy.wait_send()


def sum_over_seq(part):
    seq_count = lax.axis_size("seq")
    sems = pltpu.SemaphoreType.DMA
    return pl.pallas_call(
        lambda *refs: sum_kernel(seq_count, *refs),
        out_shape=jax.ShapeDtypeStruct(part.shape, part.dtype),
        in_specs=[in_vmem],
        out_specs=in_vmem,
        scratch_shapes=[pltpu.VMEM((seq_count,) + part.shape, part.dtype), sems((seq_count,)), sems((seq_count,))],
        compiler_params=pltpu.CompilerParams(collective_id=2, has_side_effects=True),
        name="sum_over_seq",
    )(part)


def reduce_kernel(seq_count, dp_count, part, vec, returned, vec_out, got, total, vec_dp, vec_row, vec_seq,
                  dp_send, dp_recv, seq_send, seq_recv, va_send, va_recv, vb_send, vb_recv,
                  vc_send, vc_recv, vd_send, vd_recv):
    here, row = lax.axis_index("seq"), lax.axis_index("dp")
    greet(("seq", "dp"))
    hops = range(1, dp_count)
    steps = range(1, seq_count)

    def dp_copy(step, hop):
        piece = beyond("seq", step)
        peer = beyond("dp", hop)
        return push(part.at[peer, piece], got.at[hop, piece], dp_send.at[step, hop], dp_recv.at[step, hop], "dp", peer)

    first = [push(vec.at[beyond("dp", hop)], vec_dp.at[hop], va_send.at[hop], va_recv.at[hop], "dp", beyond("dp", hop)) for hop in hops]
    for copy in first:
        copy.start()

    def launch(step, _):
        for hop in hops:
            dp_copy(lax.rem(step, seq_count), hop).start()
        return 0

    lax.fori_loop(1, seq_count + 1, launch, 0)
    for copy in first:
        copy.wait_recv()
    sums = vec[row]
    for hop in hops:
        sums = sums + vec_dp[hop]
    vec_row[...] = sums
    second = [push(vec_row.at[beyond("seq", step)], vec_seq.at[step], vb_send.at[step], vb_recv.at[step], "seq", beyond("seq", step)) for step in steps]
    for copy in second:
        copy.start()
    for copy in second:
        copy.wait_recv()
    final = vec_row[here]
    for step in steps:
        final = final + vec_seq[step]
    vec_out[row, here] = final

    def third(step, slot):
        return push(vec_out.at[row, here], vec_out.at[row, slot], vc_send.at[step], vc_recv.at[step], "seq", beyond("seq", step))

    for step in steps:
        third(step, here).start()

    def seq_copy(step, slot):
        piece = beyond("seq", step)
        return push(total.at[piece], returned.at[slot], seq_send.at[step], seq_recv.at[step], "seq", piece)

    def combined(step):
        piece = beyond("seq", step)
        for hop in hops:
            dp_copy(step, hop).wait_recv()
        value = part[row, piece].astype(f32)
        for hop in hops:
            value = value + got[hop, piece].astype(f32)
        return value.astype(bf16)

    def exchange(step, _):
        total[beyond("seq", step)] = combined(step)
        seq_copy(step, here).start()
        return 0

    lax.fori_loop(1, seq_count, exchange, 0)
    returned[here] = combined(0)

    for step in steps:
        third(step, beyond("seq", -step)).wait_recv()

    def fourth(hop, slot):
        return push(vec_out.at[row], vec_out.at[slot], vd_send.at[hop], vd_recv.at[hop], "dp", beyond("dp", hop))

    for hop in hops:
        fourth(hop, row).start()

    def finish(step, _):
        seq_copy(step, beyond("seq", -step)).wait_recv()
        seq_copy(step, here).wait_send()
        return 0

    lax.fori_loop(1, seq_count, finish, 0)

    def drain(step, _):
        for hop in hops:
            dp_copy(step, hop).wait_send()
        return 0

    lax.fori_loop(0, seq_count, drain, 0)
    for hop in hops:
        fourth(hop, beyond("dp", -hop)).wait_recv()
        fourth(hop, row).wait_send()
    for copy in first + second:
        copy.wait_send()
    for step in steps:
        third(step, here).wait_send()


def reduce_weights(part, vec):
    seq_count, dp_count = lax.axis_size("seq"), lax.axis_size("dp")
    sems = pltpu.SemaphoreType.DMA
    piece = part.shape[2:]
    lump = vec.shape[2:]
    pairs = [(seq_count, dp_count)] * 2 + [(seq_count,)] * 2 + [(dp_count,)] * 2 + [(seq_count,)] * 4 + [(dp_count,)] * 2
    return pl.pallas_call(
        lambda *refs: reduce_kernel(seq_count, dp_count, *refs),
        out_shape=[jax.ShapeDtypeStruct((seq_count,) + piece, bf16), jax.ShapeDtypeStruct(vec.shape, f32)],
        in_specs=[in_vmem] * 2,
        out_specs=[in_vmem] * 2,
        scratch_shapes=[
            pltpu.VMEM((dp_count, seq_count) + piece, bf16),
            pltpu.VMEM((seq_count,) + piece, bf16),
            pltpu.VMEM((dp_count, seq_count) + lump, f32),
            pltpu.VMEM((seq_count,) + lump, f32),
            pltpu.VMEM((seq_count,) + lump, f32),
        ]
        + [sems(pair) for pair in pairs],
        compiler_params=pltpu.CompilerParams(collective_id=3, has_side_effects=True),
        name="reduce_weights",
    )(part, vec)


def body(tokens, cotangent, doc_ids, in_weight, out_weight, in_m, in_v, out_m, out_v, vec_params, vec_m, vec_v):
    seq_count = lax.axis_size("seq")
    place = lax.axis_index("seq")
    heads = H // seq_count
    width = DI // seq_count
    mixed_width = width + 2 * N
    owner_rows = in_weight.shape[0]
    inputs = tokens[0]
    upstream_f = cotangent[0]
    local_len = inputs.shape[0]
    norm_gain = vec_params[:D]

    def by_place(matrix):
        return matrix.reshape(matrix.shape[0], seq_count, -1).transpose(1, 0, 2)

    in_low = in_weight.astype(bf16)
    out_low = out_weight.astype(bf16)
    shared = jnp.broadcast_to(in_low[None, :, 2 * DI : DI + CONV], (seq_count, owner_rows, 2 * N))
    steps = jnp.pad(by_place(in_low[:, DI + CONV :]), ((0, 0), (0, 0), (0, LANES - heads)))
    blocks = jnp.concatenate(
        [by_place(in_low[:, :DI]), by_place(in_low[:, DI : 2 * DI]), shared, steps, by_place(out_low)], axis=2
    )
    normed = input_norm(inputs, norm_gain).astype(bf16)
    upstream = upstream_f.astype(bf16)
    weights = spread_weights(blocks).reshape(D, -1)
    weights, late_vec, late_ids = lax.optimization_barrier((weights, vec_params, doc_ids))
    _, gate_gain, conv_kernel, conv_bias, step_bias, log_rate, skip_gain = unpack(late_vec)
    normed_all = lax.all_gather(normed, "seq", axis=0, tiled=True)
    upstream_all = lax.all_gather(upstream, "seq", axis=0, tiled=True)
    in_width = width + mixed_width + LANES
    in_work = weights[:, :in_width]
    out_work = weights[:, in_width:]

    ids = late_ids[0]
    ext_ids = jnp.concatenate([jnp.full((KW - 1,), -1, jnp.int32), ids])
    meta = position_table(ids)
    ids_row = ids.astype(f32)[None, :]

    def own(vector, size):
        return lax.dynamic_slice_in_dim(vector, place * size, size, vector.ndim - 1)

    own_gate_gain = own(gate_gain, width)
    own_kernel = jnp.concatenate([own(conv_kernel[:, :DI], width), conv_kernel[:, DI:]], axis=1)
    own_cbias = jnp.concatenate([own(conv_bias[:DI], width), conv_bias[DI:]])
    own_skip = own(skip_gain, heads)
    small = jnp.pad(jnp.stack([own(step_bias, heads), own(log_rate, heads)]), ((0, 6), (0, LANES - heads)))
    wide_skip = jnp.repeat(own_skip, P_SIZE)[None, :]

    projected = jnp.dot(normed_all, in_work, preferred_element_type=f32)
    gate_in = projected[:, :width]
    conv_in = projected[:, width : width + mixed_width].astype(bf16)
    step_raw = projected[:, width + mixed_width :]
    padded = jnp.concatenate([jnp.zeros((KW - 1, mixed_width), bf16), conv_in]).astype(f32)
    mixed = conv_silu(padded, own_kernel, own_cbias, ext_ids).astype(bf16)
    ssd, entries = ssd_forward(heads, mixed, step_raw, meta, ids_row, small)

    values = mixed[:, :width].astype(f32)
    ssd_out = ssd + wide_skip * values
    gate_sig = jax.nn.sigmoid(gate_in)
    gate_act = gate_in * gate_sig
    product = ssd_out * gate_act
    raw_out = (product * own_gate_gain[None, :]).astype(bf16)
    out_part = contract(raw_out, out_work, 1, 1).astype(bf16)
    out_part, upstream_all = lax.optimization_barrier((out_part, upstream_all))
    out_sum = lax.psum_scatter(out_part, "seq", scatter_dimension=0, tiled=True)
    grad_gated = jnp.dot(upstream_all, out_work, preferred_element_type=f32)
    scaled_grad = grad_gated * own_gate_gain[None, :]
    stats = jnp.stack([jnp.sum(product * product, axis=1), jnp.sum(scaled_grad * product, axis=1)])
    stats = sum_over_seq(stats.reshape(-1, LANES)).reshape(2, -1)
    scale = lax.rsqrt(stats[0] / DI + norm_eps)
    pull = scale * scale * scale * stats[1] / DI
    own_scale = lax.dynamic_slice_in_dim(scale, place * local_len, local_len)
    grad_product = scaled_grad * scale[:, None] - product * pull[:, None]
    grad_ssd = grad_product * gate_act
    grad_gate_in = grad_product * ssd_out * (gate_sig * (1.0 + gate_in * (1.0 - gate_sig)))
    grad_gate_gain = jnp.sum(grad_gated * product * scale[:, None], axis=0)
    normed_out = (raw_out.astype(f32) * scale[:, None]).astype(bf16)
    out_grad_part = contract(upstream_all, normed_out, 0, 0)

    grad_mixed, grad_raw, totals = ssd_backward(
        heads, mixed, step_raw, meta, ids_row, small, wide_skip, ssd, entries, grad_ssd
    )
    _, conv_back = jax.vjp(
        lambda block, kernel, constant: conv_silu(block, kernel, constant, ext_ids), padded, own_kernel, own_cbias
    )
    grad_padded, grad_kernel, grad_cbias = conv_back(grad_mixed)
    grad_proj = jnp.concatenate([grad_gate_in, grad_padded[KW - 1 :], grad_raw], axis=1).astype(bf16)
    grad_proj, out_sum = lax.optimization_barrier((grad_proj, out_sum))
    grad_normed_part = contract(grad_proj, in_work, 1, 1).astype(bf16)
    in_grad_part = contract(normed_all, grad_proj, 0, 0)
    grad_normed = lax.psum_scatter(grad_normed_part, "seq", scatter_dimension=0, tiled=True).astype(f32)
    outputs = inputs + out_sum.astype(f32) * own_scale[:, None]
    weight_part = jnp.concatenate([in_grad_part, out_grad_part], axis=1).astype(bf16)
    grad_norm_gain = jnp.sum(in_work.astype(f32) * in_grad_part, axis=1) / norm_gain

    def placed(part, full, size):
        return lax.dynamic_update_slice_in_dim(
            jnp.zeros(part.shape[:-1] + (full,), f32), part, place * size, part.ndim - 1
        )

    vector = repack(
        grad_norm_gain,
        placed(grad_gate_gain, DI, width),
        jnp.concatenate([placed(grad_kernel[:, :width], DI, width), grad_kernel[:, width:]], axis=1),
        jnp.concatenate([placed(grad_cbias[:width], DI, width), grad_cbias[width:]]),
        placed(totals[0, :heads], H, heads),
        placed(totals[1, :heads], H, heads),
        placed(totals[2, :heads], H, heads),
    )
    dp_count = lax.axis_size("dp")
    devices = dp_count * seq_count
    lines = -(-vector.shape[0] // (devices * LANES))
    packed = jnp.pad(vector, (0, devices * lines * LANES - vector.shape[0]))
    returned, vec_sum = reduce_weights(
        weight_part.reshape(dp_count, seq_count, owner_rows, -1), packed.reshape(dp_count, seq_count, lines, LANES)
    )
    returned = returned.astype(f32)
    vec_grad = vec_sum.reshape(-1)[: vector.shape[0]]

    def gathered(start, size):
        return returned[:, :, start : start + size].transpose(1, 0, 2).reshape(owner_rows, -1)

    in_grad = jnp.concatenate(
        [
            gathered(0, width),
            gathered(width, width),
            jnp.sum(returned[:, :, 2 * width : 2 * width + 2 * N], axis=0),
            gathered(width + mixed_width, heads),
        ],
        axis=1,
    )
    out_grad = gathered(in_width, width)

    _, norm_back = jax.vjp(lambda block: input_norm(block, norm_gain), inputs)
    (grad_inputs,) = norm_back(grad_normed)
    in_new, in_m_new, in_v_new = adamw_update(in_weight, in_grad, in_m, in_v)
    out_new, out_m_new, out_v_new = adamw_update(out_weight, out_grad, out_m, out_v)
    vec_new, vec_m_new, vec_v_new = adamw_update(vec_params, vec_grad, vec_m, vec_v)
    return (
        outputs[None],
        (upstream_f + grad_inputs)[None],
        in_grad,
        out_grad,
        vec_grad,
        in_new,
        out_new,
        vec_new,
        in_m_new,
        in_v_new,
        out_m_new,
        out_v_new,
        vec_m_new,
        vec_v_new,
    )


def solution(mesh):
    in_specs = (
        P("dp", "seq", None),
        P("dp", "seq", None),
        P("dp", None),
        P(("dp", "seq"), None),
        P(("dp", "seq"), None),
        P(("dp", "seq"), None),
        P(("dp", "seq"), None),
        P(("dp", "seq"), None),
        P(("dp", "seq"), None),
        P(),
        P(),
        P(),
    )
    out_specs = (
        P("dp", "seq", None),
        P("dp", "seq", None),
        P(("dp", "seq"), None),
        P(("dp", "seq"), None),
        P(),
        P(("dp", "seq"), None),
        P(("dp", "seq"), None),
        P(),
        P(("dp", "seq"), None),
        P(("dp", "seq"), None),
        P(("dp", "seq"), None),
        P(("dp", "seq"), None),
        P(),
        P(),
    )
    return jax.shard_map(body, mesh=mesh, in_specs=in_specs, out_specs=out_specs, check_vma=False)
```
